32 devices in a mesh: tok: 16 (over z, y, x), mdl: 2 (over core).
Axes of the slice: x: 2, y: 2, z: 4, core: 2. Of those that a mesh axis runs over, the one named last changes fastest.
Arguments:
- tokens: bfloat16 [64, 64, 768], P('tok'), may hold values from -6 to 6
- cotangent: bfloat16 [64, 64, 768], P('tok'), may hold values from -6 to 6
- norm_gain: float32 [768], replicated, may hold values from 0.5 to 1.5
- w_qkv: bfloat16 [768, 1536], P(None, 'mdl'), may hold values from -0.21875 to 0.21875
- w_out: bfloat16 [512, 768], P('mdl'), may hold values from -0.25 to 0.25
- w_up: bfloat16 [768, 3072], P(None, 'mdl'), may hold values from -0.21875 to 0.21875
- w_down: bfloat16 [3072, 768], P('mdl'), may hold values from -0.109375 to 0.109375
- w_disp: bfloat16 [768, 192], replicated, may hold values from -0.21875 to 0.21875
- rel_bias: float32 [8, 64, 448], P('mdl'), may hold values from -4 to 304
- face_source: int32 [64, 6], P('tok'), may hold values from 0 to 15, all different within a row; in each aligned block of 4 rows (0 to 3, 4 to 7, ...) at most 2 rows name the same one
- face_live: int32 [64, 6], P('tok'), may hold values 0 or 1
- send_bricks: int32 [16, 16, 2], P('tok'), may hold values from 0 to 3
Outputs:
- folding: float32 [64, 64], P('tok')
- grad_tokens: bfloat16 [64, 64, 768], P('tok')
- grad_wqkv: float32 [768, 1536], P('tok', 'mdl')
The draws below stay inside these ranges and needn't reach their ends.
Inputs may be any that keep to these rules, and one draw needn't show every extreme that they name: `face_source`: entry [b, j] names the device whose message carries the j-th face neighbour of brick b; the entries of a row differ; among the rows of one device no device is named more than 2 times, and that count is reached in every draw.
All inputs are finite; a program needn't handle non-finite values. No bound on the sum of `face_live` on one device may be relied on, other than what follows from the above.
Results may differ from the reference program's by a relative error of at most 0.015.
Values may be sent and summed in bfloat16 or wider, within the bound.
A program may use at most 64 MiB of HBM per device.

```python
import math
import jax
import jax.numpy as jnp
import numpy as np
from jax import lax

D = 768
HEADS = 8
DH = 64
FF = 3072
BT = 64
VOX = 64
FACES = 6
NBR = 7
BR_DEV = 4
CAP = 2
BRICKS = 64
N_TOK = 16


def draw_rel_bias(key, part):
    key_base = jax.random.fold_in(key, 0)
    columns = NBR * BT
    bias_shape = (HEADS, BT, columns)
    bias_base = jnp.clip(jax.random.normal(key_base, bias_shape, jnp.float32), -4.0, 4.0)
    return bias_base


def set_ends(entries, key, low, largest):
    spot = [jax.random.randint(jax.random.fold_in(key, axis), (), 0, length) for axis, length in enumerate(entries.shape)]
    longest = entries.shape.index(max(entries.shape))
    next_to = spot[:longest] + [(spot[longest] + 1) % entries.shape[longest]] + spot[longest + 1:]
    return entries.at[tuple(spot)].set(low).at[tuple(next_to)].set(largest)


def spiked(drawn, rng, source, target, blocks, factor):
    def block_of(dim):
        return (jnp.arange(drawn.shape[dim]) // (drawn.shape[dim] // blocks)).reshape((-1,) + (1,) * (drawn.ndim - 1 - dim))

    near = jax.random.permutation(rng, blocks)[block_of(target)]
    second = (block_of(target) + blocks // 2) % blocks
    return jnp.where((block_of(source) == near) | (block_of(source) == second), factor * drawn, drawn)


def block_levels(stream_key, shape, cuts, least, high):
    loudness = 1.0
    for dim, parts in cuts:
        steps = jax.random.uniform(jax.random.fold_in(jax.random.fold_in(stream_key, 6), dim), (parts,), jnp.float32, least / len(cuts), high / len(cuts))
        loudness = loudness * jnp.repeat(jnp.exp(steps), shape[dim] // parts).reshape((-1,) + (1,) * (len(shape) - 1 - dim))
    return loudness


def deal_out(stream_key, own, number, rows, count, top, most, slope):
    sequence = jax.random.permutation(stream_key, count)
    heavy_load, common = shares(count, rows * top, most, slope, True), shares(count, rows * top, most, slope, False)
    places = jnp.arange(count)

    def named(lengths, turn):
        used = int((lengths > 0).sum())
        fixed = max(1, used // 4)
        moved = fixed + (places - fixed + turn * (used - fixed)) % max(1, count - fixed)
        return jnp.zeros((count,), jnp.int32).at[sequence[jnp.where(places < fixed, places, moved)]].set(jnp.asarray(lengths, jnp.int32))

    lengths = jnp.where(number % 4 == 0, named(heavy_load, number // 4), named(common, number - number // 4 - 1))
    mixed = jax.random.permutation(jax.random.fold_in(own, 3), count)
    giver, taker = mixed[0:count // 2 * 2:2], mixed[1:count // 2 * 2:2]
    margin = jnp.minimum(lengths[giver] - 1, most - lengths[taker]) // 2
    margin = jnp.where((giver == sequence[0]) | (taker == sequence[0]) | (lengths[taker] == 0), 0, jnp.maximum(margin, 0))
    moved = jax.random.randint(jax.random.fold_in(own, 4), (count // 2,), 0, 1 << 20) % (margin + 1)
    lengths = lengths.at[giver].add(-moved).at[taker].add(moved)
    members = jnp.searchsorted(jnp.cumsum(lengths), jnp.arange(rows * top), side="right").astype(jnp.int32)
    grid = members.reshape(top, rows).T
    grid = grid[jax.random.permutation(jax.random.fold_in(own, 1), rows)]
    turn = jax.random.randint(jax.random.fold_in(own, 2), (rows, 1), 0, top)
    return jnp.take_along_axis(grid, (jnp.arange(top)[None, :] + turn) % top, axis=1)


def shares(amount, total, most, skew, full):
    weights = [(1 << 20) // math.isqrt(grade ** skew) + 1 for grade in range(1, amount + 1)]
    largest = most if full else min(most, max(-(-total // amount), total * weights[0] // sum(weights)))
    least = 1 if total - largest >= amount - 1 else 0
    counts, rest = [largest] + [least] * (amount - 1), total - largest - least * (amount - 1)
    while rest > 0:
        movable = [i for i in range(1, amount) if counts[i] < largest] or [i for i in range(1, amount) if counts[i] < most]
        pool, budget = sum([weights[i] for i in movable]), rest
        for i in movable:
            more = min(most - counts[i], max(1, budget * weights[i] // pool), rest)
            counts[i] = counts[i] + more
            rest = rest - more
    return np.array(counts)


def normal_values(own_key, dims, deviation, most, cuts=(), kind=jnp.bfloat16):
    result = jax.random.normal(own_key, dims, jnp.float32) * deviation
    if len(cuts) > 0:
        result = block_levels(own_key, dims, cuts, -0.22, 0.18) * result
    return jnp.clip(result, min=-most, max=most).astype(kind)


def gaussian_with(own_key, dims, deviation, reach, shards, heavy, held_as=jnp.bfloat16):
    values = deviation * jax.random.normal(own_key, dims, jnp.float32)
    if shards:
        values = values * block_levels(own_key, dims, shards, -0.22, 0.18)
    return jnp.clip(spiked(values, jax.random.fold_in(own_key, 3), *heavy), -reach, reach).astype(held_as)


def setup_inputs(seed: int = 0) -> dict:
    splits = jax.random.split(jax.random.key(seed), 13)
    tokens = normal_values(splits[0], (BRICKS, BT, D), 1.0, 6.0, ((0, 16),))
    cotangent = gaussian_with(splits[1], (BRICKS, BT, D), 1.0, 6.0, ((0, 16),), (0, 2, 16, 2.0))
    norm_gain = jnp.clip(1.0 + 0.1 * jax.random.normal(splits[2], (D,), jnp.float32), 0.5, 1.5)
    w_qkv = normal_values(splits[3], (D, HEADS * 3 * DH), D ** -0.5, 0.21875, ((1, 2),))
    w_out = normal_values(splits[4], (HEADS * DH, D), (HEADS * DH) ** -0.5, 0.25, ((0, 2),))
    w_up = normal_values(splits[5], (D, FF), D ** -0.5, 0.21875, ((1, 2),))
    w_down = normal_values(splits[6], (FF, D), FF ** -0.5, 0.109375, ((0, 2),))
    w_disp = normal_values(splits[7], (D, 3 * VOX), D ** -0.5, 0.21875)
    rel_bias = draw_rel_bias(jax.random.fold_in(splits[12], 71), 0)
    face_source_keys = jax.random.split(jax.random.fold_in(splits[9], 1), BRICKS // BR_DEV)
    face_source_turns = jax.random.permutation(jax.random.fold_in(splits[9], 3), BRICKS // BR_DEV)
    face_source = jax.vmap(lambda own, number: deal_out(jax.random.fold_in(splits[9], 2), own, number, BR_DEV, N_TOK, FACES, CAP, 2))(face_source_keys, face_source_turns).reshape((BRICKS, FACES))
    face_live = set_ends((jax.random.randint(splits[10], (BRICKS, FACES), 0, 4) < 3).astype(jnp.int32), jax.random.fold_in(splits[10], 1), 0, 1)
    send_bricks = set_ends(jax.random.randint(splits[11], (N_TOK, N_TOK, CAP), 0, BR_DEV), jax.random.fold_in(splits[11], 1), 0, BR_DEV - 1).astype(jnp.int32)
    return dict(tokens=tokens, cotangent=cotangent, norm_gain=norm_gain, w_qkv=w_qkv, w_out=w_out, w_up=w_up, w_down=w_down, w_disp=w_disp, rel_bias=rel_bias, face_source=face_source, face_live=face_live, send_bricks=send_bricks)


fold_weight = 8.0
norm_eps = 1e-05

def fold_of(displace):
    grid_field = displace.reshape(displace.shape[0], 3, 4, 4, 4)
    corner = grid_field[:, :, :3, :3, :3]
    slope_x = grid_field[:, :, :3, :3, 1:] - corner
    slope_y = grid_field[:, :, :3, 1:, :3] - corner
    slope_z = grid_field[:, :, 1:, :3, :3] - corner
    slopes = (slope_x, slope_y, slope_z)
    jacobian = [[slopes[across][:, target] + (1.0 if target == across else 0.0) for across in range(3)] for target in range(3)]
    determinant = jacobian[0][0] * (jacobian[1][1] * jacobian[2][2] - jacobian[1][2] * jacobian[2][1]) - jacobian[0][1] * (jacobian[1][0] * jacobian[2][2] - jacobian[1][2] * jacobian[2][0]) + jacobian[0][2] * (jacobian[1][0] * jacobian[2][1] - jacobian[1][1] * jacobian[2][0])
    return lax.optimization_barrier(jnp.mean(jax.nn.softplus(-determinant), axis=(1, 2, 3)))

def gelu_tanh(value):
    return jax.nn.gelu(value, approximate=True)

def soften(raw_scores, bias, visible, score_scale):
    scores = raw_scores * score_scale + bias[None]
    scores = jnp.where(visible[:, None, None, :], scores, -1000000000.0)
    row_max = lax.optimization_barrier(jnp.max(scores, axis=-1, keepdims=True))
    exponent = jnp.exp(scores - row_max)
    probability = exponent / lax.optimization_barrier(jnp.sum(exponent, axis=-1, keepdims=True))
    return (probability, probability.astype(jnp.bfloat16))

def reference(tokens, cotangent, norm_gain, w_qkv, w_out, w_up, w_down, w_disp, rel_bias, face_source, face_live, send_bricks):
    bricks, per_brick, model_width = tokens.shape
    row_count = bricks * per_brick
    head_count = rel_bias.shape[0]
    head_size = w_out.shape[0] // head_count
    face_count = face_source.shape[1]
    window_count = face_count + 1
    device_count = send_bricks.shape[0]
    own_bricks = bricks // device_count
    score_scale = 1.0 / math.sqrt(head_size)
    inputs = tokens.astype(jnp.float32)
    inverse = lax.rsqrt(lax.optimization_barrier(jnp.mean(inputs * inputs, axis=-1, keepdims=True)) + norm_eps)
    normed = inputs * inverse
    hidden = (normed * norm_gain).astype(jnp.bfloat16).reshape(row_count, model_width)
    packed = jnp.dot(hidden, w_qkv, preferred_element_type=jnp.float32).astype(jnp.bfloat16)
    packed = packed.reshape(bricks, per_brick, head_count, 3, head_size)
    queries = packed[:, :, :, 0]
    keyval = packed[:, :, :, 1:]
    sources = face_source.reshape(device_count, own_bricks * face_count)
    matches = (sources[:, :, None] == jnp.arange(device_count, dtype=jnp.int32)[None, None, :]).astype(jnp.int32)
    earlier = jnp.cumsum(matches, axis=1) - matches
    slot_index = lax.optimization_barrier(jnp.sum(earlier * matches, axis=2)).astype(jnp.int32)
    receiver = jnp.broadcast_to(jnp.arange(device_count, dtype=jnp.int32)[:, None], sources.shape)
    owned_index = send_bricks[sources, receiver, slot_index]
    neighbour = (sources * own_bricks + owned_index).reshape(bricks, face_count).astype(jnp.int32)
    window_ids = jnp.concatenate([jnp.arange(bricks, dtype=jnp.int32)[:, None], neighbour], axis=1)
    visible = jnp.concatenate([jnp.ones((bricks, 1), jnp.int32), face_live], axis=1) > 0
    visible = jnp.repeat(visible, per_brick, axis=1)
    windows = keyval[window_ids].reshape(bricks, window_count * per_brick, head_count, 2, head_size)
    key_rows = windows[:, :, :, 0]
    value_rows = windows[:, :, :, 1]

    def by_device(array):
        return array.reshape((device_count, own_bricks) + array.shape[1:])

    def forward_block(block):
        query_block, key_block, value_block, visible_block = block
        raw_scores = jnp.einsum('bqhd,bkhd->bhqk', query_block.astype(jnp.float32), key_block.astype(jnp.float32))
        probability, weights = soften(raw_scores, rel_bias, visible_block, score_scale)
        return jnp.einsum('bhqk,bkhd->bqhd', weights.astype(jnp.float32), value_block.astype(jnp.float32)).astype(jnp.bfloat16)
    attended = lax.map(forward_block, (by_device(queries), by_device(key_rows), by_device(value_rows), by_device(visible)))
    attended = attended.reshape(row_count, head_count * head_size)
    up_pre = jnp.dot(hidden, w_up, preferred_element_type=jnp.float32)
    activ = gelu_tanh(up_pre).astype(jnp.bfloat16)
    attn_part = jnp.dot(attended, w_out, preferred_element_type=jnp.float32)
    ffn_part = jnp.dot(activ, w_down, preferred_element_type=jnp.float32)
    layer_out = (inputs.reshape(row_count, model_width) + attn_part + ffn_part).astype(jnp.bfloat16)
    displace = jnp.dot(layer_out, w_disp, preferred_element_type=jnp.float32)
    folding, fold_back = jax.vjp(fold_of, displace)
    grad_disp = fold_back(jnp.full_like(folding, fold_weight))[0].astype(jnp.bfloat16)
    grad_out = (cotangent.reshape(row_count, model_width).astype(jnp.float32) + jnp.dot(grad_disp, w_disp.T, preferred_element_type=jnp.float32)).astype(jnp.bfloat16)
    grad_act = jnp.dot(grad_out, w_down.T, preferred_element_type=jnp.float32)
    _, gelu_back = jax.vjp(gelu_tanh, up_pre)
    grad_pre = gelu_back(grad_act)[0].astype(jnp.bfloat16)
    grad_mixed = jnp.dot(grad_out, w_out.T, preferred_element_type=jnp.float32).astype(jnp.bfloat16)
    grad_mixed = grad_mixed.reshape(bricks, per_brick, head_count, head_size)

    def backward_block(block):
        query_block, key_block, value_block, visible_block, grad_block = block
        raw_scores = jnp.einsum('bqhd,bkhd->bhqk', query_block.astype(jnp.float32), key_block.astype(jnp.float32))
        probability, weights = soften(raw_scores, rel_bias, visible_block, score_scale)
        grad_probs = jnp.einsum('bqhd,bkhd->bhqk', grad_block.astype(jnp.float32), value_block.astype(jnp.float32))
        grad_scores = probability * (grad_probs - lax.optimization_barrier(jnp.sum(probability * grad_probs, axis=-1, keepdims=True)))
        grad_low = grad_scores.astype(jnp.bfloat16).astype(jnp.float32)
        grad_query = jnp.einsum('bhqk,bkhd->bqhd', grad_low, key_block.astype(jnp.float32)) * score_scale
        grad_key = jnp.einsum('bhqk,bqhd->bkhd', grad_low, query_block.astype(jnp.float32)) * score_scale
        grad_value = jnp.einsum('bhqk,bqhd->bkhd', weights.astype(jnp.float32), grad_block.astype(jnp.float32))
        return (grad_query, grad_key, grad_value)
    grad_query, grad_key, grad_value = lax.map(backward_block, (by_device(queries), by_device(key_rows), by_device(value_rows), by_device(visible), by_device(grad_mixed)))
    grad_query = grad_query.reshape(bricks, per_brick, head_count, head_size)
    grad_window = jnp.stack([grad_key, grad_value], axis=4)
    grad_window = grad_window.reshape(bricks * window_count, per_brick, head_count, 2, head_size)
    grad_keyval = jax.ops.segment_sum(grad_window, window_ids.reshape(-1), num_segments=bricks)
    grad_packed = jnp.concatenate([grad_query[:, :, :, None], grad_keyval], axis=3).astype(jnp.bfloat16)
    grad_packed = grad_packed.reshape(row_count, head_count * 3 * head_size)
    grad_hidden = jnp.dot(grad_packed, w_qkv.T, preferred_element_type=jnp.float32) + jnp.dot(grad_pre, w_up.T, preferred_element_type=jnp.float32)
    grad_normed = grad_hidden.reshape(bricks, per_brick, model_width) * norm_gain
    grad_inputs = grad_out.reshape(bricks, per_brick, model_width).astype(jnp.float32) + inverse * (grad_normed - normed * lax.optimization_barrier(jnp.mean(grad_normed * normed, axis=-1, keepdims=True)))
    grad_weight = jnp.dot(hidden.T, grad_packed, preferred_element_type=jnp.float32)
    return (folding.reshape(bricks, per_brick), grad_inputs.astype(jnp.bfloat16), grad_weight)
```

```python
import functools
import math

import jax
import jax.numpy as jnp
from jax import lax
from jax.experimental import pallas as pl
from jax.experimental.pallas import tpu as pltpu
from jax.sharding import PartitionSpec as P

fold_weight = 8.0
norm_eps = 1e-05
F32 = jnp.float32
BF16 = jnp.bfloat16
VM = pl.BlockSpec(memory_space=pltpu.VMEM)
SM = pl.BlockSpec(memory_space=pltpu.SMEM)
PARAMS = pltpu.CompilerParams(vmem_limit_bytes=40 << 20)


def dot_nn(a, b):
    return lax.dot_general(a, b, (((1,), (0,)), ((), ())), preferred_element_type=F32)


def dot_nt(a, b):
    return lax.dot_general(a, b, (((1,), (1,)), ((), ())), preferred_element_type=F32)


def dot_tn(a, b):
    return lax.dot_general(a, b, (((0,), (0,)), ((), ())), preferred_element_type=F32)


def gelu_tanh(value):
    return jax.nn.gelu(value, approximate=True)


def project_kernel(heads, dh, send, tok, gain, w, hidden, packed, outgoing, pairs):
    bricks, per, width = tok.shape
    x = tok[...].reshape(bricks * per, width).astype(F32)
    inv = lax.rsqrt(jnp.mean(x * x, axis=-1, keepdims=True) + norm_eps)
    h = (x * inv * gain[...]).astype(BF16)
    hidden[...] = h
    pk = dot_nn(h, w[...]).astype(BF16)
    packed[...] = pk
    for b in range(bricks):
        for n in range(heads):
            pairs[b, :, n * 2 * dh : (n + 1) * 2 * dh] = pk[
                b * per : (b + 1) * per, n * 3 * dh + dh : (n + 1) * 3 * dh
            ]

    def put(s, c):
        outgoing[s] = pairs[send[s]]
        return c

    lax.fori_loop(0, outgoing.shape[0], put, 0)


def fill_window(arrival, packed, incoming, window, b, heads, dh, per, faces):
    for n in range(heads):
        window[0:per, n * 2 * dh : (n + 1) * 2 * dh] = packed[
            b * per : (b + 1) * per, n * 3 * dh + dh : (n + 1) * 3 * dh
        ]
    for j in range(faces):
        window[(j + 1) * per : (j + 2) * per, :] = incoming[arrival[b * faces + j]]


def forward_kernel(heads, dh, per, faces, arrival, packed, incoming, bias, seen, attended, probs, window):
    bricks = packed.shape[0] // per
    scale = 1.0 / math.sqrt(dh)
    for b in range(bricks):
        fill_window(arrival, packed, incoming, window, b, heads, dh, per, faces)
        live = seen[b : b + 1, :] > 0
        rows = slice(b * per, (b + 1) * per)
        for n in range(heads):
            q = packed[rows, n * 3 * dh : n * 3 * dh + dh]
            k = window[:, n * 2 * dh : n * 2 * dh + dh]
            v = window[:, n * 2 * dh + dh : (n + 1) * 2 * dh]
            s = dot_nt(q, k) * scale + bias[n]
            s = jnp.where(live, s, -1000000000.0)
            e = jnp.exp(s - jnp.max(s, axis=-1, keepdims=True))
            p = e * (1.0 / jnp.sum(e, axis=-1, keepdims=True))
            probs[b * heads + n] = p
            attended[rows, n * dh : (n + 1) * dh] = dot_nn(p.astype(BF16), v).astype(BF16)


def backward_kernel(
    heads, dh, per, faces, arrival, packed, incoming, probs, mixed, gquery, gown, returning, window, gwin
):
    bricks = packed.shape[0] // per
    scale = 1.0 / math.sqrt(dh)

    def clear(s, c):
        returning[s] = jnp.zeros(returning.shape[1:], BF16)
        return c

    lax.fori_loop(0, returning.shape[0], clear, 0)
    for b in range(bricks):
        fill_window(arrival, packed, incoming, window, b, heads, dh, per, faces)
        rows = slice(b * per, (b + 1) * per)
        for n in range(heads):
            q = packed[rows, n * 3 * dh : n * 3 * dh + dh]
            k = window[:, n * 2 * dh : n * 2 * dh + dh]
            v = window[:, n * 2 * dh + dh : (n + 1) * 2 * dh]
            p = probs[b * heads + n]
            g = mixed[rows, n * dh : (n + 1) * dh]
            dp = dot_nt(g, v)
            ds = p * (dp - jnp.sum(p * dp, axis=-1, keepdims=True))
            low = ds.astype(BF16)
            gquery[rows, n * dh : (n + 1) * dh] = dot_nn(low, k) * scale
            gwin[:, n * 2 * dh : n * 2 * dh + dh] = dot_tn(low, q) * scale
            gwin[:, n * 2 * dh + dh : (n + 1) * 2 * dh] = dot_tn(p.astype(BF16), g)
        gown[b] = gwin[0:per, :]
        for j in range(faces):
            returning[arrival[b * faces + j]] = gwin[(j + 1) * per : (j + 2) * per, :].astype(BF16)


def collect_kernel(heads, dh, send, returned, gquery, gown, gpacked, acc):
    bricks, per, _ = gown.shape
    acc[...] = gown[...]

    def add(s, c):
        acc[send[s]] += returned[s].astype(F32)
        return c

    lax.fori_loop(0, returned.shape[0], add, 0)
    for b in range(bricks):
        rows = slice(b * per, (b + 1) * per)
        for n in range(heads):
            gpacked[rows, n * 3 * dh : n * 3 * dh + dh] = gquery[rows, n * dh : (n + 1) * dh].astype(BF16)
            gpacked[rows, n * 3 * dh + dh : (n + 1) * 3 * dh] = acc[
                b, :, n * 2 * dh : (n + 1) * 2 * dh
            ].astype(BF16)


def swap(src, dst, send_sem, recv_sem):
    other = 1 - lax.axis_index("mdl")
    barrier = pltpu.get_barrier_semaphore()
    pl.semaphore_signal(barrier, inc=1, device_id={"mdl": other}, device_id_type=pl.DeviceIdType.MESH)
    pl.semaphore_wait(barrier, 1)
    copy = pltpu.make_async_remote_copy(
        src_ref=src,
        dst_ref=dst,
        send_sem=send_sem,
        recv_sem=recv_sem,
        device_id={"mdl": other},
        device_id_type=pl.DeviceIdType.MESH,
    )
    copy.start()
    return copy


def fold_math(x, total, cot, w_disp, folding, grad_out):
    out = (x.astype(F32) + total).astype(BF16)
    disp = lax.dot_general(w_disp, out, (((0,), (1,)), ((), ())), preferred_element_type=F32)
    vox = disp.shape[0] // 3
    steps = (1, 4, 16)
    comp = [disp[c * vox : (c + 1) * vox] for c in range(3)]
    row = lax.broadcasted_iota(jnp.int32, comp[0].shape, 0)
    inside = ((row & 3) < 3) & (((row >> 2) & 3) < 3) & ((row >> 4) < 3)
    jac = [
        [
            pltpu.roll(comp[i], vox - steps[k], 0) - comp[i] + (1.0 if i == k else 0.0)
            for k in range(3)
        ]
        for i in range(3)
    ]
    cof = [[None] * 3 for _ in range(3)]
    for i in range(3):
        i1, i2 = (i + 1) % 3, (i + 2) % 3
        for k in range(3):
            k1, k2 = (k + 1) % 3, (k + 2) % 3
            cof[i][k] = jac[i1][k1] * jac[i2][k2] - jac[i1][k2] * jac[i2][k1]
    det = jac[0][0] * cof[0][0] + jac[0][1] * cof[0][1] + jac[0][2] * cof[0][2]
    small = jnp.exp(-jnp.abs(det))
    soft = jnp.maximum(-det, 0.0) + jnp.log1p(small)
    folding[...] = jnp.sum(jnp.where(inside, soft, 0.0), axis=0, keepdims=True) * (1.0 / 27.0)
    sig = jnp.where(det > 0, small, 1.0) / (1.0 + small)
    coef = jnp.where(inside, sig * (-fold_weight / 27.0), 0.0)
    grads = []
    for i in range(3):
        g = jnp.zeros_like(det)
        for k in range(3):
            t = jnp.where(inside, coef * cof[i][k], 0.0)
            g = g + pltpu.roll(t, steps[k], 0) - t
        grads.append(g)
    gd = jnp.concatenate(grads, axis=0).astype(BF16)
    back = lax.dot_general(gd, w_disp, (((0,), (1,)), ((), ())), preferred_element_type=F32)
    grad_out[...] = (cot.astype(F32) + back).astype(BF16)


def fold_swap_kernel(x, part, cot, w_disp, folding, grad_out, other, send_sem, recv_sem):
    swap(part, other, send_sem, recv_sem).wait()
    fold_math(x[...], part[...] + other[...], cot[...], w_disp[...], folding, grad_out)


def fold_kernel(x, part, cot, w_disp, folding, grad_out):
    fold_math(x[...], part[...], cot[...], w_disp[...], folding, grad_out)


def norm_math(x, grad_hidden, grad_out, gain, out):
    x = x.astype(F32)
    inv = lax.rsqrt(jnp.mean(x * x, axis=-1, keepdims=True) + norm_eps)
    normed = x * inv
    g = grad_hidden * gain
    out[...] = (
        grad_out.astype(F32) + inv * (g - normed * jnp.mean(g * normed, axis=-1, keepdims=True))
    ).astype(BF16)


def norm_swap_kernel(x, part, grad_out, gain, out, other, send_sem, recv_sem):
    swap(part, other, send_sem, recv_sem).wait()
    norm_math(x[...], part[...].astype(F32) + other[...].astype(F32), grad_out[...], gain[...], out)


def norm_kernel(x, part, grad_out, gain, out):
    norm_math(x[...], part[...].astype(F32), grad_out[...], gain[...], out)


def body(
    tokens,
    cotangent,
    norm_gain,
    w_qkv,
    w_out,
    w_up,
    w_down,
    w_disp,
    rel_bias,
    face_source,
    face_live,
    send_bricks,
):
    bricks, per, width = tokens.shape
    rows = bricks * per
    heads = rel_bias.shape[0]
    dh = w_out.shape[0] // heads
    faces = face_source.shape[1]
    devices = lax.axis_size("tok")
    pair = lax.axis_size("mdl") == 2
    slots = send_bricks.shape[2]
    total = devices * slots
    kv = heads * 2 * dh
    span = (faces + 1) * per
    send = send_bricks.reshape(-1)
    sources = face_source.reshape(-1)
    matches = (sources[:, None] == sources[None, :]).astype(jnp.int32)
    count = sources.shape[0]
    before = jnp.arange(count)[None, :] < jnp.arange(count)[:, None]
    arrival = sources * slots + jnp.sum(jnp.where(before, matches, 0), axis=1)
    seen = jnp.concatenate([jnp.ones((bricks, 1), jnp.int32), face_live], axis=1)
    seen = jnp.repeat(seen, per, axis=1)
    gain = norm_gain.reshape(1, width)
    flat = tokens.reshape(rows, width)

    hidden, packed, outgoing = pl.pallas_call(
        functools.partial(project_kernel, heads, dh),
        out_shape=(
            jax.ShapeDtypeStruct((rows, width), BF16),
            jax.ShapeDtypeStruct((rows, heads * 3 * dh), BF16),
            jax.ShapeDtypeStruct((total, per, kv), BF16),
        ),
        in_specs=[SM, VM, VM, VM],
        out_specs=(VM, VM, VM),
        scratch_shapes=[pltpu.VMEM((bricks, per, kv), BF16)],
        compiler_params=PARAMS,
        name="project",
    )(send, tokens, gain, w_qkv)

    incoming = lax.all_to_all(outgoing, "tok", split_axis=0, concat_axis=0, tiled=True)

    up_pre = jnp.dot(hidden, w_up, preferred_element_type=F32)
    activ, gelu_back = jax.vjp(gelu_tanh, up_pre)
    part_ffn = jnp.dot(activ.astype(BF16), w_down, preferred_element_type=F32)

    attended, probs = pl.pallas_call(
        functools.partial(forward_kernel, heads, dh, per, faces),
        out_shape=(
            jax.ShapeDtypeStruct((rows, heads * dh), BF16),
            jax.ShapeDtypeStruct((bricks * heads, per, span), F32),
        ),
        in_specs=[SM, VM, VM, VM, VM],
        out_specs=(VM, VM),
        scratch_shapes=[pltpu.VMEM((span, kv), BF16)],
        compiler_params=PARAMS,
        name="attend",
    )(arrival, packed, incoming, rel_bias, seen)

    part_out = part_ffn + jnp.dot(attended, w_out, preferred_element_type=F32)
    fold_shape = (
        jax.ShapeDtypeStruct((1, rows), F32),
        jax.ShapeDtypeStruct((rows, width), BF16),
    )
    cot = cotangent.reshape(rows, width)
    if pair:
        folding, grad_out = pl.pallas_call(
            fold_swap_kernel,
            out_shape=fold_shape,
            in_specs=[VM] * 4,
            out_specs=(VM, VM),
            scratch_shapes=[
                pltpu.VMEM((rows, width), F32),
                pltpu.SemaphoreType.DMA,
                pltpu.SemaphoreType.DMA,
            ],
            compiler_params=pltpu.CompilerParams(
                vmem_limit_bytes=40 << 20, collective_id=0, has_side_effects=True
            ),
            name="fold_swap",
        )(flat, part_out, cot, w_disp)
    else:
        folding, grad_out = pl.pallas_call(
            fold_kernel,
            out_shape=fold_shape,
            in_specs=[VM] * 4,
            out_specs=(VM, VM),
            compiler_params=PARAMS,
            name="fold",
        )(flat, lax.psum(part_out, "mdl"), cot, w_disp)

    grad_mixed = jnp.dot(grad_out, w_out.T, preferred_element_type=F32).astype(BF16)

    gquery, gown, returning = pl.pallas_call(
        functools.partial(backward_kernel, heads, dh, per, faces),
        out_shape=(
            jax.ShapeDtypeStruct((rows, heads * dh), F32),
            jax.ShapeDtypeStruct((bricks, per, kv), F32),
            jax.ShapeDtypeStruct((total, per, kv), BF16),
        ),
        in_specs=[SM, VM, VM, VM, VM],
        out_specs=(VM, VM, VM),
        scratch_shapes=[pltpu.VMEM((span, kv), BF16), pltpu.VMEM((span, kv), F32)],
        compiler_params=PARAMS,
        name="attend_back",
    )(arrival, packed, incoming, probs, grad_mixed)

    returned = lax.all_to_all(returning, "tok", split_axis=0, concat_axis=0, tiled=True)

    grad_act = jnp.dot(grad_out, w_down.T, preferred_element_type=F32)
    grad_pre = gelu_back(grad_act)[0].astype(BF16)
    part_up = jnp.dot(grad_pre, w_up.T, preferred_element_type=F32)

    grad_packed = pl.pallas_call(
        functools.partial(collect_kernel, heads, dh),
        out_shape=jax.ShapeDtypeStruct((rows, heads * 3 * dh), BF16),
        in_specs=[SM, VM, VM, VM],
        out_specs=VM,
        scratch_shapes=[pltpu.VMEM((bricks, per, kv), F32)],
        compiler_params=PARAMS,
        name="collect",
    )(send, returned, gquery, gown)

    terms = lax.dot_general(
        hidden, grad_packed, (((0,), (0,)), ((), ())), preferred_element_type=F32
    ).astype(BF16)
    terms = terms.reshape(devices, width // devices, heads * 3 * dh)
    terms = lax.all_to_all(terms, "tok", split_axis=0, concat_axis=0, tiled=True)
    grad_weight = jnp.sum(terms.astype(F32), axis=0)

    grad_part = (part_up + jnp.dot(grad_packed, w_qkv.T, preferred_element_type=F32)).astype(BF16)
    norm_shape = jax.ShapeDtypeStruct((rows, width), BF16)
    if pair:
        grad_tokens = pl.pallas_call(
            norm_swap_kernel,
            out_shape=norm_shape,
            in_specs=[VM] * 4,
            out_specs=VM,
            scratch_shapes=[
                pltpu.VMEM((rows, width), BF16),
                pltpu.SemaphoreType.DMA,
                pltpu.SemaphoreType.DMA,
            ],
            compiler_params=pltpu.CompilerParams(
                vmem_limit_bytes=40 << 20, collective_id=1, has_side_effects=True
            ),
            name="norm_swap",
        )(flat, grad_part, grad_out, gain)
    else:
        grad_tokens = pl.pallas_call(
            norm_kernel,
            out_shape=norm_shape,
            in_specs=[VM] * 4,
            out_specs=VM,
            compiler_params=PARAMS,
            name="norm",
        )(flat, lax.psum(grad_part, "mdl"), grad_out, gain)
    return (folding.reshape(bricks, per), grad_tokens.reshape(bricks, per, width), grad_weight)


def solution(mesh):
    return jax.shard_map(
        body,
        mesh=mesh,
        in_specs=(
            P("tok", None, None),
            P("tok", None, None),
            P(),
            P(None, "mdl"),
            P("mdl", None),
            P(None, "mdl"),
            P("mdl", None),
            P(),
            P("mdl", None, None),
            P("tok", None),
            P("tok", None),
            P("tok", None, None),
        ),
        out_specs=(P("tok", None), P("tok", None, None), P("tok", "mdl")),
        check_vma=False,
    )
```

```python
import functools
import math

import jax
import jax.numpy as jnp
from jax import lax
from jax.experimental import pallas as pl
from jax.experimental.pallas import tpu as pltpu
from jax.sharding import PartitionSpec as P

fold_weight = 8.0
norm_eps = 1e-05
F32 = jnp.float32
BF16 = jnp.bfloat16
VM = pl.BlockSpec(memory_space=pltpu.VMEM)
SM = pl.BlockSpec(memory_space=pltpu.SMEM)
PARAMS = pltpu.CompilerParams(vmem_limit_bytes=40 << 20)


def dot_nn(a, b):
    return lax.dot_general(a, b, (((1,), (0,)), ((), ())), preferred_element_type=F32)


def dot_nt(a, b):
    return lax.dot_general(a, b, (((1,), (1,)), ((), ())), preferred_element_type=F32)


def dot_tn(a, b):
    return lax.dot_general(a, b, (((0,), (0,)), ((), ())), preferred_element_type=F32)


def gelu_tanh(value):
    return jax.nn.gelu(value, approximate=True)


def project_kernel(heads, dh, send, tok, gain, w, hidden, packed, outgoing, pairs):
    bricks, per, width = tok.shape
    x = tok[...].reshape(bricks * per, width).astype(F32)
    inv = lax.rsqrt(jnp.mean(x * x, axis=-1, keepdims=True) + norm_eps)
    h = (x * inv * gain[...]).astype(BF16)
    hidden[...] = h
    pk = dot_nn(h, w[...]).astype(BF16)
    packed[...] = pk
    for b in range(bricks):
        for n in range(heads):
            pairs[b, :, n * 2 * dh : (n + 1) * 2 * dh] = pk[
                b * per : (b + 1) * per, n * 3 * dh + dh : (n + 1) * 3 * dh
            ]

    def put(s, c):
        outgoing[s] = pairs[send[s]]
        return c

    lax.fori_loop(0, outgoing.shape[0], put, 0)


def fill_window(arrival, packed, incoming, window, b, heads, dh, per, faces):
    for n in range(heads):
        window[0:per, n * 2 * dh : (n + 1) * 2 * dh] = packed[
            b * per : (b + 1) * per, n * 3 * dh + dh : (n + 1) * 3 * dh
        ]
    for j in range(faces):
        window[(j + 1) * per : (j + 2) * per, :] = incoming[arrival[b * faces + j]]


def forward_kernel(heads, dh, per, faces, arrival, packed, incoming, bias, seen, attended, probs, window):
    bricks = packed.shape[0] // per
    scale = 1.0 / math.sqrt(dh)
    for b in range(bricks):
        fill_window(arrival, packed, incoming, window, b, heads, dh, per, faces)
        live = seen[b : b + 1, :] > 0
        rows = slice(b * per, (b + 1) * per)
        for n in range(heads):
            q = packed[rows, n * 3 * dh : n * 3 * dh + dh]
            k = window[:, n * 2 * dh : n * 2 * dh + dh]
            v = window[:, n * 2 * dh + dh : (n + 1) * 2 * dh]
            s = dot_nt(q, k) * scale + bias[n]
            s = jnp.where(live, s, -1000000000.0)
            e = jnp.exp(s - jnp.max(s, axis=-1, keepdims=True))
            p = e * (1.0 / jnp.sum(e, axis=-1, keepdims=True))
            probs[b * heads + n] = p
            attended[rows, n * dh : (n + 1) * dh] = dot_nn(p.astype(BF16), v).astype(BF16)


def backward_kernel(
    heads, dh, per, faces, arrival, packed, incoming, probs, mixed, gquery, gown, returning, window, gwin
):
    bricks = packed.shape[0] // per
    scale = 1.0 / math.sqrt(dh)

    def clear(s, c):
        returning[s] = jnp.zeros(returning.shape[1:], BF16)
        return c

    lax.fori_loop(0, returning.shape[0], clear, 0)
    for b in range(bricks):
        fill_window(arrival, packed, incoming, window, b, heads, dh, per, faces)
        rows = slice(b * per, (b + 1) * per)
        for n in range(heads):
            q = packed[rows, n * 3 * dh : n * 3 * dh + dh]
            k = window[:, n * 2 * dh : n * 2 * dh + dh]
            v = window[:, n * 2 * dh + dh : (n + 1) * 2 * dh]
            p = probs[b * heads + n]
            g = mixed[rows, n * dh : (n + 1) * dh]
            dp = dot_nt(g, v)
            ds = p * (dp - jnp.sum(p * dp, axis=-1, keepdims=True))
            low = ds.astype(BF16)
            gquery[rows, n * dh : (n + 1) * dh] = dot_nn(low, k) * scale
            gwin[:, n * 2 * dh : n * 2 * dh + dh] = dot_tn(low, q) * scale
            gwin[:, n * 2 * dh + dh : (n + 1) * 2 * dh] = dot_tn(p.astype(BF16), g)
        gown[b] = gwin[0:per, :]
        for j in range(faces):
            returning[arrival[b * faces + j]] = gwin[(j + 1) * per : (j + 2) * per, :].astype(BF16)


def collect_kernel(heads, dh, send, returned, gquery, gown, gpacked, acc):
    bricks, per, _ = gown.shape
    acc[...] = gown[...]

    def add(s, c):
        acc[send[s]] += returned[s].astype(F32)
        return c

    lax.fori_loop(0, returned.shape[0], add, 0)
    for b in range(bricks):
        rows = slice(b * per, (b + 1) * per)
        for n in range(heads):
            gpacked[rows, n * 3 * dh : n * 3 * dh + dh] = gquery[rows, n * dh : (n + 1) * dh].astype(BF16)
            gpacked[rows, n * 3 * dh + dh : (n + 1) * 3 * dh] = acc[
                b, :, n * 2 * dh : (n + 1) * 2 * dh
            ].astype(BF16)


def swap(src, dst, send_sem, recv_sem):
    other = 1 - lax.axis_index("mdl")
    barrier = pltpu.get_barrier_semaphore()
    pl.semaphore_signal(barrier, inc=1, device_id={"mdl": other}, device_id_type=pl.DeviceIdType.MESH)
    pl.semaphore_wait(barrier, 1)
    copy = pltpu.make_async_remote_copy(
        src_ref=src,
        dst_ref=dst,
        send_sem=send_sem,
        recv_sem=recv_sem,
        device_id={"mdl": other},
        device_id_type=pl.DeviceIdType.MESH,
    )
    copy.start()
    return copy


def fold_math(x, total, cot, w_disp, folding, grad_out):
    out = (x.astype(F32) + total).astype(BF16)
    disp = lax.dot_general(w_disp, out, (((0,), (1,)), ((), ())), preferred_element_type=F32)
    vox = disp.shape[0] // 3
    steps = (1, 4, 16)
    comp = [disp[c * vox : (c + 1) * vox] for c in range(3)]
    row = lax.broadcasted_iota(jnp.int32, comp[0].shape, 0)
    inside = ((row & 3) < 3) & (((row >> 2) & 3) < 3) & ((row >> 4) < 3)
    jac = [
        [
            pltpu.roll(comp[i], vox - steps[k], 0) - comp[i] + (1.0 if i == k else 0.0)
            for k in range(3)
        ]
        for i in range(3)
    ]
    cof = [[None] * 3 for _ in range(3)]
    for i in range(3):
        i1, i2 = (i + 1) % 3, (i + 2) % 3
        for k in range(3):
            k1, k2 = (k + 1) % 3, (k + 2) % 3
            cof[i][k] = jac[i1][k1] * jac[i2][k2] - jac[i1][k2] * jac[i2][k1]
    det = jac[0][0] * cof[0][0] + jac[0][1] * cof[0][1] + jac[0][2] * cof[0][2]
    small = jnp.exp(-jnp.abs(det))
    soft = jnp.maximum(-det, 0.0) + jnp.log1p(small)
    folding[...] = jnp.sum(jnp.where(inside, soft, 0.0), axis=0, keepdims=True) * (1.0 / 27.0)
    sig = jnp.where(det > 0, small, 1.0) / (1.0 + small)
    coef = jnp.where(inside, sig * (-fold_weight / 27.0), 0.0)
    grads = []
    for i in range(3):
        g = jnp.zeros_like(det)
        for k in range(3):
            t = jnp.where(inside, coef * cof[i][k], 0.0)
            g = g + pltpu.roll(t, steps[k], 0) - t
        grads.append(g)
    gd = jnp.concatenate(grads, axis=0).astype(BF16)
    back = lax.dot_general(gd, w_disp, (((0,), (1,)), ((), ())), preferred_element_type=F32)
    grad_out[...] = (cot.astype(F32) + back).astype(BF16)


def fold_swap_kernel(x, part, cot, w_disp, folding, grad_out, other, send_sem, recv_sem):
    swap(part, other, send_sem, recv_sem).wait()
    fold_math(x[...], part[...] + other[...], cot[...], w_disp[...], folding, grad_out)


def fold_kernel(x, part, cot, w_disp, folding, grad_out):
    fold_math(x[...], part[...], cot[...], w_disp[...], folding, grad_out)


def norm_math(x, grad_hidden, grad_out, gain, out):
    x = x.astype(F32)
    inv = lax.rsqrt(jnp.mean(x * x, axis=-1, keepdims=True) + norm_eps)
    normed = x * inv
    g = grad_hidden * gain
    out[...] = (
        grad_out.astype(F32) + inv * (g - normed * jnp.mean(g * normed, axis=-1, keepdims=True))
    ).astype(BF16)


def norm_swap_kernel(x, part, grad_out, gain, out, other, send_sem, recv_sem):
    swap(part, other, send_sem, recv_sem).wait()
    norm_math(x[...], part[...].astype(F32) + other[...].astype(F32), grad_out[...], gain[...], out)


def norm_kernel(x, part, grad_out, gain, out):
    norm_math(x[...], part[...].astype(F32), grad_out[...], gain[...], out)


def body_wide(
    tokens,
    cotangent,
    norm_gain,
    w_qkv,
    w_out,
    w_up,
    w_down,
    w_disp,
    rel_bias,
    face_source,
    face_live,
    send_bricks,
):
    bricks, per, width = tokens.shape
    rows = bricks * per
    heads = rel_bias.shape[0]
    dh = w_out.shape[0] // heads
    faces = face_source.shape[1]
    devices = lax.axis_size("tok")
    pair = lax.axis_size("mdl") == 2
    slots = send_bricks.shape[2]
    total = devices * slots
    kv = heads * 2 * dh
    span = (faces + 1) * per
    send = send_bricks.reshape(-1)
    sources = face_source.reshape(-1)
    matches = (sources[:, None] == sources[None, :]).astype(jnp.int32)
    count = sources.shape[0]
    before = jnp.arange(count)[None, :] < jnp.arange(count)[:, None]
    arrival = sources * slots + jnp.sum(jnp.where(before, matches, 0), axis=1)
    seen = jnp.concatenate([jnp.ones((bricks, 1), jnp.int32), face_live], axis=1)
    seen = jnp.repeat(seen, per, axis=1)
    gain = norm_gain.reshape(1, width)
    flat = tokens.reshape(rows, width)

    hidden, packed, outgoing = pl.pallas_call(
        functools.partial(project_kernel, heads, dh),
        out_shape=(
            jax.ShapeDtypeStruct((rows, width), BF16),
            jax.ShapeDtypeStruct((rows, heads * 3 * dh), BF16),
            jax.ShapeDtypeStruct((total, per, kv), BF16),
        ),
        in_specs=[SM, VM, VM, VM],
        out_specs=(VM, VM, VM),
        scratch_shapes=[pltpu.VMEM((bricks, per, kv), BF16)],
        compiler_params=PARAMS,
        name="project",
    )(send, tokens, gain, w_qkv)

    incoming = lax.all_to_all(outgoing, "tok", split_axis=0, concat_axis=0, tiled=True)

    up_pre = jnp.dot(hidden, w_up, preferred_element_type=F32)
    activ, gelu_back = jax.vjp(gelu_tanh, up_pre)
    part_ffn = jnp.dot(activ.astype(BF16), w_down, preferred_element_type=F32)

    attended, probs = pl.pallas_call(
        functools.partial(forward_kernel, heads, dh, per, faces),
        out_shape=(
            jax.ShapeDtypeStruct((rows, heads * dh), BF16),
            jax.ShapeDtypeStruct((bricks * heads, per, span), F32),
        ),
        in_specs=[SM, VM, VM, VM, VM],
        out_specs=(VM, VM),
        scratch_shapes=[pltpu.VMEM((span, kv), BF16)],
        compiler_params=PARAMS,
        name="attend",
    )(arrival, packed, incoming, rel_bias, seen)

    part_out = part_ffn + jnp.dot(attended, w_out, preferred_element_type=F32)
    fold_shape = (
        jax.ShapeDtypeStruct((1, rows), F32),
        jax.ShapeDtypeStruct((rows, width), BF16),
    )
    cot = cotangent.reshape(rows, width)
    if pair:
        folding, grad_out = pl.pallas_call(
            fold_swap_kernel,
            out_shape=fold_shape,
            in_specs=[VM] * 4,
            out_specs=(VM, VM),
            scratch_shapes=[
                pltpu.VMEM((rows, width), F32),
                pltpu.SemaphoreType.DMA,
                pltpu.SemaphoreType.DMA,
            ],
            compiler_params=pltpu.CompilerParams(
                vmem_limit_bytes=40 << 20, collective_id=0, has_side_effects=True
            ),
            name="fold_swap",
        )(flat, part_out, cot, w_disp)
    else:
        folding, grad_out = pl.pallas_call(
            fold_kernel,
            out_shape=fold_shape,
            in_specs=[VM] * 4,
            out_specs=(VM, VM),
            compiler_params=PARAMS,
            name="fold",
        )(flat, lax.psum(part_out, "mdl"), cot, w_disp)

    grad_mixed = jnp.dot(grad_out, w_out.T, preferred_element_type=F32).astype(BF16)

    gquery, gown, returning = pl.pallas_call(
        functools.partial(backward_kernel, heads, dh, per, faces),
        out_shape=(
            jax.ShapeDtypeStruct((rows, heads * dh), F32),
            jax.ShapeDtypeStruct((bricks, per, kv), F32),
            jax.ShapeDtypeStruct((total, per, kv), BF16),
        ),
        in_specs=[SM, VM, VM, VM, VM],
        out_specs=(VM, VM, VM),
        scratch_shapes=[pltpu.VMEM((span, kv), BF16), pltpu.VMEM((span, kv), F32)],
        compiler_params=PARAMS,
        name="attend_back",
    )(arrival, packed, incoming, probs, grad_mixed)

    returned = lax.all_to_all(returning, "tok", split_axis=0, concat_axis=0, tiled=True)

    grad_act = jnp.dot(grad_out, w_down.T, preferred_element_type=F32)
    grad_pre = gelu_back(grad_act)[0].astype(BF16)
    part_up = jnp.dot(grad_pre, w_up.T, preferred_element_type=F32)

    grad_packed = pl.pallas_call(
        functools.partial(collect_kernel, heads, dh),
        out_shape=jax.ShapeDtypeStruct((rows, heads * 3 * dh), BF16),
        in_specs=[SM, VM, VM, VM],
        out_specs=VM,
        scratch_shapes=[pltpu.VMEM((bricks, per, kv), F32)],
        compiler_params=PARAMS,
        name="collect",
    )(send, returned, gquery, gown)

    terms = lax.dot_general(
        hidden, grad_packed, (((0,), (0,)), ((), ())), preferred_element_type=F32
    ).astype(BF16)
    terms = terms.reshape(devices, width // devices, heads * 3 * dh)
    terms = lax.all_to_all(terms, "tok", split_axis=0, concat_axis=0, tiled=True)
    grad_weight = jnp.sum(terms.astype(F32), axis=0)

    grad_part = (part_up + jnp.dot(grad_packed, w_qkv.T, preferred_element_type=F32)).astype(BF16)
    norm_shape = jax.ShapeDtypeStruct((rows, width), BF16)
    if pair:
        grad_tokens = pl.pallas_call(
            norm_swap_kernel,
            out_shape=norm_shape,
            in_specs=[VM] * 4,
            out_specs=VM,
            scratch_shapes=[
                pltpu.VMEM((rows, width), BF16),
                pltpu.SemaphoreType.DMA,
                pltpu.SemaphoreType.DMA,
            ],
            compiler_params=pltpu.CompilerParams(
                vmem_limit_bytes=40 << 20, collective_id=1, has_side_effects=True
            ),
            name="norm_swap",
        )(flat, grad_part, grad_out, gain)
    else:
        grad_tokens = pl.pallas_call(
            norm_kernel,
            out_shape=norm_shape,
            in_specs=[VM] * 4,
            out_specs=VM,
            compiler_params=PARAMS,
            name="norm",
        )(flat, lax.psum(grad_part, "mdl"), grad_out, gain)
    return (folding.reshape(bricks, per), grad_tokens.reshape(bricks, per, width), grad_weight)


def gelu_slope(u):
    c = math.sqrt(2.0 / math.pi)
    t = jnp.tanh(c * (u + 0.044715 * (u * u * u)))
    return 0.5 * (1.0 + t) + 0.5 * u * (1.0 - t * t) * c * (1.0 + (3.0 * 0.044715) * (u * u))


def remote(src, dst, send_sem, recv_sem, where):
    return pltpu.make_async_remote_copy(
        src_ref=src,
        dst_ref=dst,
        send_sem=send_sem,
        recv_sem=recv_sem,
        device_id=where,
        device_id_type=pl.DeviceIdType.MESH,
    )


def greet(me, count, other):
    barrier = pltpu.get_barrier_semaphore()

    def hail(i, c):
        peer = lax.rem(me + i + 1, count)
        pl.semaphore_signal(barrier, inc=1, device_id={"tok": peer}, device_id_type=pl.DeviceIdType.MESH)
        return c

    lax.fori_loop(0, count - 1, hail, 0)
    pl.semaphore_signal(barrier, inc=1, device_id={"mdl": other}, device_id_type=pl.DeviceIdType.MESH)
    pl.semaphore_wait(barrier, count)


def gather_kernel(
    count, send, tok, gain, wq_hbm, wup_hbm, wdn_hbm,
    recv, hidden, packed, up_pre, part,
    msg, wq, wup, wdn, wsem, ssem, rsem, fssem, frsem,
):
    me, core = lax.axis_index("tok"), lax.axis_index("mdl")
    other = 1 - core
    bricks, per, width = tok.shape
    slots = recv.shape[1]
    half = per // 2
    mine = pl.ds(pl.multiple_of(core * half, half), half)
    theirs = pl.ds(pl.multiple_of(other * half, half), half)
    loads = [
        pltpu.make_async_copy(a, b, wsem.at[i])
        for i, (a, b) in enumerate(((wq_hbm, wq), (wup_hbm, wup), (wdn_hbm, wdn)))
    ]
    for load in loads:
        load.start()
    greet(me, count, other)

    def out_copy(i):
        peer = lax.rem(me + i + 1, count)
        return remote(msg.at[i], recv.at[me, :, mine, :], ssem.at[i], rsem.at[i], {"tok": peer})

    def launch(i, c):
        peer = lax.rem(me + i + 1, count)
        for k in range(slots):
            msg[i, k] = tok[send[peer * slots + k], mine, :]
        out_copy(i).start()
        return c

    lax.fori_loop(0, count - 1, launch, 0)
    for k in range(slots):
        recv[me, k] = tok[send[me * slots + k]]
    x = tok[...].reshape(bricks * per, width).astype(F32)
    inv = lax.rsqrt(jnp.mean(x * x, axis=-1, keepdims=True) + norm_eps)
    hidden[...] = (x * inv * gain[...]).astype(BF16)
    loads[0].wait()
    packed[...] = dot_nn(hidden[...], wq[...]).astype(BF16)
    loads[1].wait()
    loads[2].wait()
    ff = wup.shape[1]
    step = ff // 3
    for n in range(3):
        cols = slice(n * step, (n + 1) * step)
        u = dot_nn(hidden[...], wup[:, cols])
        up_pre[:, cols] = u
        term = dot_nn(gelu_tanh(u).astype(BF16), wdn[cols, :])
        part[...] = term if n == 0 else part[...] + term

    def relay_copy(i, rows):
        source = lax.rem(me - (i + 1) + count, count)
        block = recv.at[source, :, rows, :]
        return remote(block, block, fssem.at[i], frsem.at[i], {"mdl": other})

    def relay(i, c):
        source = lax.rem(me - (i + 1) + count, count)
        remote(msg.at[i], recv.at[source, :, mine, :], ssem.at[i], rsem.at[i], {"tok": source}).wait_recv()
        relay_copy(i, mine).start()
        return c

    lax.fori_loop(0, count - 1, relay, 0)

    def finish(i, c):
        out_copy(i).wait_send()
        relay_copy(i, mine).wait_send()
        relay_copy(i, theirs).wait_recv()
        return c

    lax.fori_loop(0, count - 1, finish, 0)


def attend_kernel(
    heads, dh, per, faces, arrival, hidden, packed, recv, gain, wq, bias, seen,
    attended, probs, window, hid, near,
):
    bricks = packed.shape[0] // per
    scale = 1.0 / math.sqrt(dh)
    for b in range(bricks):
        rows = slice(b * per, (b + 1) * per)
        for j in range(faces):
            near[j * per : (j + 1) * per, :] = recv[arrival[b * faces + j]]
        x = near[...].astype(F32)
        inv = lax.rsqrt(jnp.mean(x * x, axis=-1, keepdims=True) + norm_eps)
        h = (x * inv * gain[...]).astype(BF16)
        hid[b, 0:per, :] = hidden[rows, :]
        hid[b, per:, :] = h
        pk = dot_nn(h, wq[...]).astype(BF16)
        for n in range(heads):
            two = slice(n * 2 * dh, (n + 1) * 2 * dh)
            window[b, 0:per, two] = packed[rows, n * 3 * dh + dh : (n + 1) * 3 * dh]
            window[b, per:, two] = pk[:, n * 3 * dh + dh : (n + 1) * 3 * dh]
        live = seen[b : b + 1, :] > 0
        for n in range(heads):
            q = packed[rows, n * 3 * dh : n * 3 * dh + dh]
            k = window[b, :, n * 2 * dh : n * 2 * dh + dh]
            v = window[b, :, n * 2 * dh + dh : (n + 1) * 2 * dh]
            s = dot_nt(q, k) * scale + bias[n]
            s = jnp.where(live, s, -1000000000.0)
            e = jnp.exp(s - jnp.max(s, axis=-1, keepdims=True))
            p = e * (1.0 / jnp.sum(e, axis=-1, keepdims=True))
            probs[b * heads + n] = p
            attended[rows, n * dh : (n + 1) * dh] = dot_nn(p.astype(BF16), v).astype(BF16)


def attend_back_kernel(
    heads, dh, per, faces, arrival, packed, window, hid, probs, mixed, wq,
    own, ret, gw, gp, acc,
):
    bricks = packed.shape[0] // per
    scale = 1.0 / math.sqrt(dh)

    def clear(s, c):
        ret[s] = jnp.zeros(ret.shape[1:], BF16)
        return c

    lax.fori_loop(0, ret.shape[0], clear, 0)
    gp[...] = jnp.zeros(gp.shape, BF16)
    for b in range(bricks):
        rows = slice(b * per, (b + 1) * per)
        for n in range(heads):
            q = packed[rows, n * 3 * dh : n * 3 * dh + dh]
            k = window[b, :, n * 2 * dh : n * 2 * dh + dh]
            v = window[b, :, n * 2 * dh + dh : (n + 1) * 2 * dh]
            p = probs[b * heads + n]
            g = mixed[rows, n * dh : (n + 1) * dh]
            dp = dot_nt(g, v)
            low = (p * (dp - jnp.sum(p * dp, axis=-1, keepdims=True))).astype(BF16)
            at = n * 3 * dh
            gp[0:per, at : at + dh] = (dot_nn(low, k) * scale).astype(BF16)
            gp[:, at + dh : at + 2 * dh] = (dot_tn(low, q) * scale).astype(BF16)
            gp[:, at + 2 * dh : at + 3 * dh] = dot_tn(p.astype(BF16), g).astype(BF16)
        back = dot_nt(gp[...], wq[...])
        own[rows, :] = back[0:per]
        for j in range(faces):
            ret[arrival[b * faces + j]] = back[(j + 1) * per : (j + 2) * per].astype(BF16)
        term = dot_tn(hid[b], gp[...])
        acc[...] = term if b == 0 else acc[...] + term
    gw[...] = acc[...].astype(BF16)


def return_kernel(
    count, send, tok, gain, gout, own, ret, gw, up_pre, wup_hbm, wdn_hbm,
    out, gw_out,
    sib, msg, inbox, part, pmsg, pbox, result, g1a, g1b, s1a, s1b, g2a, g2b, s2, g3, wup, wdn,
    wsem, bs, br, ssem, rsem, xs, xr,
):
    me, core = lax.axis_index("tok"), lax.axis_index("mdl")
    other = 1 - core
    bricks, per, width = tok.shape
    slots = ret.shape[1]
    half = per // 2
    mine = pl.ds(pl.multiple_of(core * half, half), half)
    theirs = pl.ds(pl.multiple_of(other * half, half), half)
    x, y, z = lax.rem(me, 2), lax.rem(me // 2, 2), me // 4
    xn, yn = me + 1 - 2 * x, me + 2 - 4 * y
    loads = [
        pltpu.make_async_copy(a, b, wsem.at[i])
        for i, (a, b) in enumerate(((wup_hbm, wup), (wdn_hbm, wdn)))
    ]
    for load in loads:
        load.start()
    greet(me, count, other)
    cut = gw.shape[-1] // 2

    def sib_copy(i):
        peer = lax.rem(me + i, count)
        return remote(ret.at[peer, :, theirs, :], sib.at[i], bs.at[i], br.at[i], {"mdl": other})

    def give(i, c):
        sib_copy(i).start()
        return c

    lax.fori_loop(0, count, give, 0)
    one_a = remote(gw.at[:, :, 1 - x, :, pl.ds(0, cut)], g1a, xs.at[0], xr.at[0], {"tok": xn})
    one_b = remote(gw.at[:, 1 - y, :, :, pl.ds(cut, cut)], g1b, xs.at[1], xr.at[1], {"tok": yn})

    def out_copy(i):
        peer = lax.rem(me + i, count)
        return remote(msg.at[i], inbox.at[i], ssem.at[i], rsem.at[i], {"tok": peer})

    def launch(i, c):
        peer = lax.rem(me + i, count)
        sib_copy(i).wait()
        msg[i] = (ret[peer, :, mine, :].astype(F32) + sib[i].astype(F32)).astype(BF16)
        out_copy(i).start()
        return c

    one_a.start()
    one_b.start()
    lax.fori_loop(1, count, launch, 0)
    sib_copy(0).wait()
    inbox[0] = (ret[me, :, mine, :].astype(F32) + sib[0].astype(F32)).astype(BF16)

    for load in loads:
        load.wait()
    ff = wup.shape[1]
    step = ff // 3

    def feed(n):
        cols = slice(n * step, (n + 1) * step)
        act = dot_nt(gout[...], wdn[cols, :])
        pre = (gelu_slope(up_pre[:, cols]) * act).astype(BF16)
        term = dot_nt(pre, wup[:, cols])
        part[...] = part[...] + term

    part[...] = own[...]
    feed(0)
    feed(1)
    one_a.wait()
    one_b.wait()
    s1a[...] = (gw[:, :, x, :, 0:cut].astype(F32) + g1a[...].astype(F32)).astype(BF16)
    s1b[...] = (gw[:, y, :, :, cut : 2 * cut].astype(F32) + g1b[...].astype(F32)).astype(BF16)
    two_a = remote(s1a.at[:, 1 - y], g2a, xs.at[2], xr.at[2], {"tok": yn})
    two_b = remote(s1b.at[:, 1 - x], g2b, xs.at[3], xr.at[3], {"tok": xn})
    two_a.start()
    two_b.start()
    feed(2)
    for b in range(bricks):
        pmsg[b] = part[pl.ds(pl.multiple_of(b * per + other * half, half), half), :].astype(BF16)
    swap_part = remote(pmsg, pbox, xs.at[4], xr.at[4], {"mdl": other})
    swap_part.start()
    two_a.wait()
    two_b.wait()
    s2[:, :, 0:cut] = (s1a[:, y].astype(F32) + g2a[...].astype(F32)).astype(BF16)
    s2[:, :, cut : 2 * cut] = (s1b[:, x].astype(F32) + g2b[...].astype(F32)).astype(BF16)
    last = []
    for d in range(1, 4):
        copy = remote(
            s2.at[lax.rem(z + d, 4)], g3.at[d - 1], xs.at[5 + d], xr.at[5 + d],
            {"tok": lax.rem(me + 4 * d, count)},
        )
        copy.start()
        last.append(copy)
    swap_part.wait()
    for b in range(bricks):
        result[b] = part[pl.ds(pl.multiple_of(b * per + core * half, half), half), :] + pbox[b].astype(F32)

    def take(i, c):
        source = lax.rem(me - i + count, count)

        @pl.when(i > 0)
        def _():
            remote(msg.at[i], inbox.at[i], ssem.at[i], rsem.at[i], {"tok": source}).wait()

        for k in range(slots):
            value = inbox[i, k].astype(F32)
            brick = send[source * slots + k]
            for b in range(bricks):
                result[b] = result[b] + jnp.where(brick == b, 1.0, 0.0) * value
        return c

    lax.fori_loop(0, count, take, 0)
    for b in range(bricks):
        v = tok[b, mine, :].astype(F32)
        inv = lax.rsqrt(jnp.mean(v * v, axis=-1, keepdims=True) + norm_eps)
        normed = v * inv
        g = result[b] * gain[...]
        base = gout[pl.ds(pl.multiple_of(b * per + core * half, half), half), :].astype(F32)
        out[b, mine, :] = (
            base + inv * (g - normed * jnp.mean(g * normed, axis=-1, keepdims=True))
        ).astype(BF16)
    share = remote(out.at[:, mine, :], out.at[:, mine, :], xs.at[5], xr.at[5], {"mdl": other})
    share.start()
    for copy in last:
        copy.wait()
    gw_out[...] = (
        s2[z].astype(F32) + g3[0].astype(F32) + g3[1].astype(F32) + g3[2].astype(F32)
    )
    share.wait_send()
    remote(out.at[:, theirs, :], out.at[:, theirs, :], xs.at[5], xr.at[5], {"mdl": other}).wait_recv()


def body(
    tokens,
    cotangent,
    norm_gain,
    w_qkv,
    w_out,
    w_up,
    w_down,
    w_disp,
    rel_bias,
    face_source,
    face_live,
    send_bricks,
):
    bricks, per, width = tokens.shape
    rows = bricks * per
    heads = rel_bias.shape[0]
    dh = w_out.shape[0] // heads
    faces = face_source.shape[1]
    devices = lax.axis_size("tok")
    slots = send_bricks.shape[2]
    total = devices * slots
    kv = heads * 2 * dh
    wide = heads * 3 * dh
    span = (faces + 1) * per
    ff = w_up.shape[1]
    half = per // 2
    send = send_bricks.reshape(-1)
    sources = face_source.reshape(-1)
    matches = (sources[:, None] == sources[None, :]).astype(jnp.int32)
    count = sources.shape[0]
    before = jnp.arange(count)[None, :] < jnp.arange(count)[:, None]
    arrival = sources * slots + jnp.sum(jnp.where(before, matches, 0), axis=1)
    seen = jnp.concatenate([jnp.ones((bricks, 1), jnp.int32), face_live], axis=1)
    seen = jnp.repeat(seen, per, axis=1)
    gain = norm_gain.reshape(1, width)
    flat = tokens.reshape(rows, width)
    any_spec = pl.BlockSpec(memory_space=pl.ANY)
    dma = pltpu.SemaphoreType.DMA

    def shape(dims, kind=BF16):
        return jax.ShapeDtypeStruct(dims, kind)

    def talk(ident):
        return pltpu.CompilerParams(
            vmem_limit_bytes=48 << 20, collective_id=ident, has_side_effects=True
        )

    recv, hidden, packed, up_pre, part_ffn = pl.pallas_call(
        functools.partial(gather_kernel, devices),
        out_shape=(
            shape((devices, slots, per, width)),
            shape((rows, width)),
            shape((rows, wide)),
            shape((rows, ff), F32),
            shape((rows, width), F32),
        ),
        in_specs=[SM, VM, VM, any_spec, any_spec, any_spec],
        out_specs=(VM,) * 5,
        scratch_shapes=[
            pltpu.VMEM((devices - 1, slots, half, width), BF16),
            pltpu.VMEM((width, wide), BF16),
            pltpu.VMEM((width, ff), BF16),
            pltpu.VMEM((ff, width), BF16),
            dma((3,)),
            dma((devices - 1,)),
            dma((devices - 1,)),
            dma((devices - 1,)),
            dma((devices - 1,)),
        ],
        compiler_params=talk(2),
        name="gather",
    )(send, tokens, gain, w_qkv, w_up, w_down)

    attended, probs, window, hid = pl.pallas_call(
        functools.partial(attend_kernel, heads, dh, per, faces),
        out_shape=(
            shape((rows, heads * dh)),
            shape((bricks * heads, per, span), F32),
            shape((bricks, span, kv)),
            shape((bricks, span, width)),
        ),
        in_specs=[SM] + [VM] * 7,
        out_specs=(VM,) * 4,
        scratch_shapes=[pltpu.VMEM((faces * per, width), BF16)],
        compiler_params=PARAMS,
        name="attend",
    )(arrival, hidden, packed, recv.reshape(total, per, width), gain, w_qkv, rel_bias, seen)

    part_out = part_ffn + jnp.dot(attended, w_out, preferred_element_type=F32)
    folding, grad_out = pl.pallas_call(
        fold_swap_kernel,
        out_shape=(shape((1, rows), F32), shape((rows, width))),
        in_specs=[VM] * 4,
        out_specs=(VM, VM),
        scratch_shapes=[pltpu.VMEM((rows, width), F32), dma, dma],
        compiler_params=talk(0),
        name="fold_swap",
    )(flat, part_out, cotangent.reshape(rows, width), w_disp)
    grad_mixed = jnp.dot(grad_out, w_out.T, preferred_element_type=F32).astype(BF16)

    own, ret, gw = pl.pallas_call(
        functools.partial(attend_back_kernel, heads, dh, per, faces),
        out_shape=(
            shape((rows, width), F32),
            shape((total, per, width)),
            shape((width, wide)),
        ),
        in_specs=[SM] + [VM] * 6,
        out_specs=(VM,) * 3,
        scratch_shapes=[pltpu.VMEM((span, wide), BF16), pltpu.VMEM((width, wide), F32)],
        compiler_params=PARAMS,
        name="attend_back",
    )(arrival, packed, window, hid, probs, grad_mixed, w_qkv)

    piece = width // devices
    cut = wide // 2
    grad_tokens, grad_weight = pl.pallas_call(
        functools.partial(return_kernel, devices),
        out_shape=(shape((bricks, per, width)), shape((piece, wide), F32)),
        in_specs=[SM] + [VM] * 7 + [any_spec] * 2,
        out_specs=(VM, VM),
        scratch_shapes=[
            pltpu.VMEM((devices, slots, half, width), BF16),
            pltpu.VMEM((devices, slots, half, width), BF16),
            pltpu.VMEM((devices, slots, half, width), BF16),
            pltpu.VMEM((rows, width), F32),
            pltpu.VMEM((bricks, half, width), BF16),
            pltpu.VMEM((bricks, half, width), BF16),
            pltpu.VMEM((bricks, half, width), F32),
            pltpu.VMEM((4, 2, piece, cut), BF16),
            pltpu.VMEM((4, 2, piece, cut), BF16),
            pltpu.VMEM((4, 2, piece, cut), BF16),
            pltpu.VMEM((4, 2, piece, cut), BF16),
            pltpu.VMEM((4, piece, cut), BF16),
            pltpu.VMEM((4, piece, cut), BF16),
            pltpu.VMEM((4, piece, wide), BF16),
            pltpu.VMEM((3, piece, wide), BF16),
            pltpu.VMEM((width, ff), BF16),
            pltpu.VMEM((ff, width), BF16),
            dma((2,)),
            dma((devices,)),
            dma((devices,)),
            dma((devices,)),
            dma((devices,)),
            dma((9,)),
            dma((9,)),
        ],
        compiler_params=talk(1),
        name="give_back",
    )(
        send,
        tokens,
        gain,
        grad_out,
        own,
        ret.reshape(devices, slots, per, width),
        gw.reshape(4, 2, 2, piece, wide),
        up_pre,
        w_up,
        w_down,
    )
    return (folding.reshape(bricks, per), grad_tokens, grad_weight)


def solution(mesh):
    return jax.shard_map(
        body if mesh.shape["tok"] == 16 and mesh.shape["mdl"] == 2 else body_wide,
        mesh=mesh,
        in_specs=(
            P("tok", None, None),
            P("tok", None, None),
            P(),
            P(None, "mdl"),
            P("mdl", None),
            P(None, "mdl"),
            P("mdl", None),
            P(),
            P("mdl", None, None),
            P("tok", None),
            P("tok", None),
            P("tok", None, None),
        ),
        out_specs=(P("tok", None), P("tok", None, None), P("tok", "mdl")),
        check_vma=False,
    )
```

```python
import functools
import math

import jax
import jax.numpy as jnp
from jax import lax
from jax.experimental import pallas as pl
from jax.experimental.pallas import tpu as pltpu
from jax.sharding import PartitionSpec as P

fold_weight = 8.0
norm_eps = 1e-05
F32 = jnp.float32
BF16 = jnp.bfloat16
VM = pl.BlockSpec(memory_space=pltpu.VMEM)
SM = pl.BlockSpec(memory_space=pltpu.SMEM)
PARAMS = pltpu.CompilerParams(vmem_limit_bytes=40 << 20)


def dot_nn(a, b):
    return lax.dot_general(a, b, (((1,), (0,)), ((), ())), preferred_element_type=F32)


def dot_nt(a, b):
    return lax.dot_general(a, b, (((1,), (1,)), ((), ())), preferred_element_type=F32)


def dot_tn(a, b):
    return lax.dot_general(a, b, (((0,), (0,)), ((), ())), preferred_element_type=F32)


def gelu_tanh(value):
    return jax.nn.gelu(value, approximate=True)


def project_kernel(heads, dh, send, tok, gain, w, hidden, packed, outgoing, pairs):
    bricks, per, width = tok.shape
    x = tok[...].reshape(bricks * per, width).astype(F32)
    inv = lax.rsqrt(jnp.mean(x * x, axis=-1, keepdims=True) + norm_eps)
    h = (x * inv * gain[...]).astype(BF16)
    hidden[...] = h
    pk = dot_nn(h, w[...]).astype(BF16)
    packed[...] = pk
    for b in range(bricks):
        for n in range(heads):
            pairs[b, :, n * 2 * dh : (n + 1) * 2 * dh] = pk[
                b * per : (b + 1) * per, n * 3 * dh + dh : (n + 1) * 3 * dh
            ]

    def put(s, c):
        outgoing[s] = pairs[send[s]]
        return c

    lax.fori_loop(0, outgoing.shape[0], put, 0)


def fill_window(arrival, packed, incoming, window, b, heads, dh, per, faces):
    for n in range(heads):
        window[0:per, n * 2 * dh : (n + 1) * 2 * dh] = packed[
            b * per : (b + 1) * per, n * 3 * dh + dh : (n + 1) * 3 * dh
        ]
    for j in range(faces):
        window[(j + 1) * per : (j + 2) * per, :] = incoming[arrival[b * faces + j]]


def forward_kernel(heads, dh, per, faces, arrival, packed, incoming, bias, seen, attended, probs, window):
    bricks = packed.shape[0] // per
    scale = 1.0 / math.sqrt(dh)
    for b in range(bricks):
        fill_window(arrival, packed, incoming, window, b, heads, dh, per, faces)
        live = seen[b : b + 1, :] > 0
        rows = slice(b * per, (b + 1) * per)
        for n in range(heads):
            q = packed[rows, n * 3 * dh : n * 3 * dh + dh]
            k = window[:, n * 2 * dh : n * 2 * dh + dh]
            v = window[:, n * 2 * dh + dh : (n + 1) * 2 * dh]
            s = dot_nt(q, k) * scale + bias[n]
            s = jnp.where(live, s, -1000000000.0)
            e = jnp.exp(s - jnp.max(s, axis=-1, keepdims=True))
            p = e * (1.0 / jnp.sum(e, axis=-1, keepdims=True))
            probs[b * heads + n] = p
            attended[rows, n * dh : (n + 1) * dh] = dot_nn(p.astype(BF16), v).astype(BF16)


def backward_kernel(
    heads, dh, per, faces, arrival, packed, incoming, probs, mixed, gquery, gown, returning, window, gwin
):
    bricks = packed.shape[0] // per
    scale = 1.0 / math.sqrt(dh)

    def clear(s, c):
        returning[s] = jnp.zeros(returning.shape[1:], BF16)
        return c

    lax.fori_loop(0, returning.shape[0], clear, 0)
    for b in range(bricks):
        fill_window(arrival, packed, incoming, window, b, heads, dh, per, faces)
        rows = slice(b * per, (b + 1) * per)
        for n in range(heads):
            q = packed[rows, n * 3 * dh : n * 3 * dh + dh]
            k = window[:, n * 2 * dh : n * 2 * dh + dh]
            v = window[:, n * 2 * dh + dh : (n + 1) * 2 * dh]
            p = probs[b * heads + n]
            g = mixed[rows, n * dh : (n + 1) * dh]
            dp = dot_nt(g, v)
            ds = p * (dp - jnp.sum(p * dp, axis=-1, keepdims=True))
            low = ds.astype(BF16)
            gquery[rows, n * dh : (n + 1) * dh] = dot_nn(low, k) * scale
            gwin[:, n * 2 * dh : n * 2 * dh + dh] = dot_tn(low, q) * scale
            gwin[:, n * 2 * dh + dh : (n + 1) * 2 * dh] = dot_tn(p.astype(BF16), g)
        gown[b] = gwin[0:per, :]
        for j in range(faces):
            returning[arrival[b * faces + j]] = gwin[(j + 1) * per : (j + 2) * per, :].astype(BF16)


def collect_kernel(heads, dh, send, returned, gquery, gown, gpacked, acc):
    bricks, per, _ = gown.shape
    acc[...] = gown[...]

    def add(s, c):
        acc[send[s]] += returned[s].astype(F32)
        return c

    lax.fori_loop(0, returned.shape[0], add, 0)
    for b in range(bricks):
        rows = slice(b * per, (b + 1) * per)
        for n in range(heads):
            gpacked[rows, n * 3 * dh : n * 3 * dh + dh] = gquery[rows, n * dh : (n + 1) * dh].astype(BF16)
            gpacked[rows, n * 3 * dh + dh : (n + 1) * 3 * dh] = acc[
                b, :, n * 2 * dh : (n + 1) * 2 * dh
            ].astype(BF16)


def swap(src, dst, send_sem, recv_sem):
    other = 1 - lax.axis_index("mdl")
    barrier = pltpu.get_barrier_semaphore()
    pl.semaphore_signal(barrier, inc=1, device_id={"mdl": other}, device_id_type=pl.DeviceIdType.MESH)
    pl.semaphore_wait(barrier, 1)
    copy = pltpu.make_async_remote_copy(
        src_ref=src,
        dst_ref=dst,
        send_sem=send_sem,
        recv_sem=recv_sem,
        device_id={"mdl": other},
        device_id_type=pl.DeviceIdType.MESH,
    )
    copy.start()
    return copy


def fold_math(x, total, cot, w_disp, folding, grad_out):
    out = (x.astype(F32) + total).astype(BF16)
    disp = lax.dot_general(w_disp, out, (((0,), (1,)), ((), ())), preferred_element_type=F32)
    vox = disp.shape[0] // 3
    steps = (1, 4, 16)
    comp = [disp[c * vox : (c + 1) * vox] for c in range(3)]
    row = lax.broadcasted_iota(jnp.int32, comp[0].shape, 0)
    inside = ((row & 3) < 3) & (((row >> 2) & 3) < 3) & ((row >> 4) < 3)
    jac = [
        [
            pltpu.roll(comp[i], vox - steps[k], 0) - comp[i] + (1.0 if i == k else 0.0)
            for k in range(3)
        ]
        for i in range(3)
    ]
    cof = [[None] * 3 for _ in range(3)]
    for i in range(3):
        i1, i2 = (i + 1) % 3, (i + 2) % 3
        for k in range(3):
            k1, k2 = (k + 1) % 3, (k + 2) % 3
            cof[i][k] = jac[i1][k1] * jac[i2][k2] - jac[i1][k2] * jac[i2][k1]
    det = jac[0][0] * cof[0][0] + jac[0][1] * cof[0][1] + jac[0][2] * cof[0][2]
    small = jnp.exp(-jnp.abs(det))
    soft = jnp.maximum(-det, 0.0) + jnp.log1p(small)
    folding[...] = jnp.sum(jnp.where(inside, soft, 0.0), axis=0, keepdims=True) * (1.0 / 27.0)
    sig = jnp.where(det > 0, small, 1.0) / (1.0 + small)
    coef = jnp.where(inside, sig * (-fold_weight / 27.0), 0.0)
    grads = []
    for i in range(3):
        g = jnp.zeros_like(det)
        for k in range(3):
            t = jnp.where(inside, coef * cof[i][k], 0.0)
            g = g + pltpu.roll(t, steps[k], 0) - t
        grads.append(g)
    gd = jnp.concatenate(grads, axis=0).astype(BF16)
    back = lax.dot_general(gd, w_disp, (((0,), (1,)), ((), ())), preferred_element_type=F32)
    grad_out[...] = (cot.astype(F32) + back).astype(BF16)


def fold_swap_kernel(x, part, cot, w_disp, folding, grad_out, other, send_sem, recv_sem):
    swap(part, other, send_sem, recv_sem).wait()
    fold_math(x[...], part[...] + other[...], cot[...], w_disp[...], folding, grad_out)


def fold_kernel(x, part, cot, w_disp, folding, grad_out):
    fold_math(x[...], part[...], cot[...], w_disp[...], folding, grad_out)


def norm_math(x, grad_hidden, grad_out, gain, out):
    x = x.astype(F32)
    inv = lax.rsqrt(jnp.mean(x * x, axis=-1, keepdims=True) + norm_eps)
    normed = x * inv
    g = grad_hidden * gain
    out[...] = (
        grad_out.astype(F32) + inv * (g - normed * jnp.mean(g * normed, axis=-1, keepdims=True))
    ).astype(BF16)


def norm_swap_kernel(x, part, grad_out, gain, out, other, send_sem, recv_sem):
    swap(part, other, send_sem, recv_sem).wait()
    norm_math(x[...], part[...].astype(F32) + other[...].astype(F32), grad_out[...], gain[...], out)


def norm_kernel(x, part, grad_out, gain, out):
    norm_math(x[...], part[...].astype(F32), grad_out[...], gain[...], out)


def body_wide(
    tokens,
    cotangent,
    norm_gain,
    w_qkv,
    w_out,
    w_up,
    w_down,
    w_disp,
    rel_bias,
    face_source,
    face_live,
    send_bricks,
):
    bricks, per, width = tokens.shape
    rows = bricks * per
    heads = rel_bias.shape[0]
    dh = w_out.shape[0] // heads
    faces = face_source.shape[1]
    devices = lax.axis_size("tok")
    pair = lax.axis_size("mdl") == 2
    slots = send_bricks.shape[2]
    total = devices * slots
    kv = heads * 2 * dh
    span = (faces + 1) * per
    send = send_bricks.reshape(-1)
    sources = face_source.reshape(-1)
    matches = (sources[:, None] == sources[None, :]).astype(jnp.int32)
    count = sources.shape[0]
    before = jnp.arange(count)[None, :] < jnp.arange(count)[:, None]
    arrival = sources * slots + jnp.sum(jnp.where(before, matches, 0), axis=1)
    seen = jnp.concatenate([jnp.ones((bricks, 1), jnp.int32), face_live], axis=1)
    seen = jnp.repeat(seen, per, axis=1)
    gain = norm_gain.reshape(1, width)
    flat = tokens.reshape(rows, width)

    hidden, packed, outgoing = pl.pallas_call(
        functools.partial(project_kernel, heads, dh),
        out_shape=(
            jax.ShapeDtypeStruct((rows, width), BF16),
            jax.ShapeDtypeStruct((rows, heads * 3 * dh), BF16),
            jax.ShapeDtypeStruct((total, per, kv), BF16),
        ),
        in_specs=[SM, VM, VM, VM],
        out_specs=(VM, VM, VM),
        scratch_shapes=[pltpu.VMEM((bricks, per, kv), BF16)],
        compiler_params=PARAMS,
        name="project",
    )(send, tokens, gain, w_qkv)

    incoming = lax.all_to_all(outgoing, "tok", split_axis=0, concat_axis=0, tiled=True)

    up_pre = jnp.dot(hidden, w_up, preferred_element_type=F32)
    activ, gelu_back = jax.vjp(gelu_tanh, up_pre)
    part_ffn = jnp.dot(activ.astype(BF16), w_down, preferred_element_type=F32)

    attended, probs = pl.pallas_call(
        functools.partial(forward_kernel, heads, dh, per, faces),
        out_shape=(
            jax.ShapeDtypeStruct((rows, heads * dh), BF16),
            jax.ShapeDtypeStruct((bricks * heads, per, span), F32),
        ),
        in_specs=[SM, VM, VM, VM, VM],
        out_specs=(VM, VM),
        scratch_shapes=[pltpu.VMEM((span, kv), BF16)],
        compiler_params=PARAMS,
        name="attend",
    )(arrival, packed, incoming, rel_bias, seen)

    part_out = part_ffn + jnp.dot(attended, w_out, preferred_element_type=F32)
    fold_shape = (
        jax.ShapeDtypeStruct((1, rows), F32),
        jax.ShapeDtypeStruct((rows, width), BF16),
    )
    cot = cotangent.reshape(rows, width)
    if pair:
        folding, grad_out = pl.pallas_call(
            fold_swap_kernel,
            out_shape=fold_shape,
            in_specs=[VM] * 4,
            out_specs=(VM, VM),
            scratch_shapes=[
                pltpu.VMEM((rows, width), F32),
                pltpu.SemaphoreType.DMA,
                pltpu.SemaphoreType.DMA,
            ],
            compiler_params=pltpu.CompilerParams(
                vmem_limit_bytes=40 << 20, collective_id=0, has_side_effects=True
            ),
            name="fold_swap",
        )(flat, part_out, cot, w_disp)
    else:
        folding, grad_out = pl.pallas_call(
            fold_kernel,
            out_shape=fold_shape,
            in_specs=[VM] * 4,
            out_specs=(VM, VM),
            compiler_params=PARAMS,
            name="fold",
        )(flat, lax.psum(part_out, "mdl"), cot, w_disp)

    grad_mixed = jnp.dot(grad_out, w_out.T, preferred_element_type=F32).astype(BF16)

    gquery, gown, returning = pl.pallas_call(
        functools.partial(backward_kernel, heads, dh, per, faces),
        out_shape=(
            jax.ShapeDtypeStruct((rows, heads * dh), F32),
            jax.ShapeDtypeStruct((bricks, per, kv), F32),
            jax.ShapeDtypeStruct((total, per, kv), BF16),
        ),
        in_specs=[SM, VM, VM, VM, VM],
        out_specs=(VM, VM, VM),
        scratch_shapes=[pltpu.VMEM((span, kv), BF16), pltpu.VMEM((span, kv), F32)],
        compiler_params=PARAMS,
        name="attend_back",
    )(arrival, packed, incoming, probs, grad_mixed)

    returned = lax.all_to_all(returning, "tok", split_axis=0, concat_axis=0, tiled=True)

    grad_act = jnp.dot(grad_out, w_down.T, preferred_element_type=F32)
    grad_pre = gelu_back(grad_act)[0].astype(BF16)
    part_up = jnp.dot(grad_pre, w_up.T, preferred_element_type=F32)

    grad_packed = pl.pallas_call(
        functools.partial(collect_kernel, heads, dh),
        out_shape=jax.ShapeDtypeStruct((rows, heads * 3 * dh), BF16),
        in_specs=[SM, VM, VM, VM],
        out_specs=VM,
        scratch_shapes=[pltpu.VMEM((bricks, per, kv), F32)],
        compiler_params=PARAMS,
        name="collect",
    )(send, returned, gquery, gown)

    terms = lax.dot_general(
        hidden, grad_packed, (((0,), (0,)), ((), ())), preferred_element_type=F32
    ).astype(BF16)
    terms = terms.reshape(devices, width // devices, heads * 3 * dh)
    terms = lax.all_to_all(terms, "tok", split_axis=0, concat_axis=0, tiled=True)
    grad_weight = jnp.sum(terms.astype(F32), axis=0)

    grad_part = (part_up + jnp.dot(grad_packed, w_qkv.T, preferred_element_type=F32)).astype(BF16)
    norm_shape = jax.ShapeDtypeStruct((rows, width), BF16)
    if pair:
        grad_tokens = pl.pallas_call(
            norm_swap_kernel,
            out_shape=norm_shape,
            in_specs=[VM] * 4,
            out_specs=VM,
            scratch_shapes=[
                pltpu.VMEM((rows, width), BF16),
                pltpu.SemaphoreType.DMA,
                pltpu.SemaphoreType.DMA,
            ],
            compiler_params=pltpu.CompilerParams(
                vmem_limit_bytes=40 << 20, collective_id=1, has_side_effects=True
            ),
            name="norm_swap",
        )(flat, grad_part, grad_out, gain)
    else:
        grad_tokens = pl.pallas_call(
            norm_kernel,
            out_shape=norm_shape,
            in_specs=[VM] * 4,
            out_specs=VM,
            compiler_params=PARAMS,
            name="norm",
        )(flat, lax.psum(grad_part, "mdl"), grad_out, gain)
    return (folding.reshape(bricks, per), grad_tokens.reshape(bricks, per, width), grad_weight)


def gelu_slope(u):
    c = math.sqrt(2.0 / math.pi)
    t = jnp.tanh(c * (u + 0.044715 * (u * u * u)))
    return 0.5 * (1.0 + t) + 0.5 * u * (1.0 - t * t) * c * (1.0 + (3.0 * 0.044715) * (u * u))


def remote(src, dst, send_sem, recv_sem, where):
    return pltpu.make_async_remote_copy(
        src_ref=src,
        dst_ref=dst,
        send_sem=send_sem,
        recv_sem=recv_sem,
        device_id=where,
        device_id_type=pl.DeviceIdType.MESH,
    )


def greet(me, count, other):
    barrier = pltpu.get_barrier_semaphore()

    def hail(i, c):
        peer = lax.rem(me + i + 1, count)
        pl.semaphore_signal(barrier, inc=1, device_id={"tok": peer}, device_id_type=pl.DeviceIdType.MESH)
        return c

    lax.fori_loop(0, count - 1, hail, 0)
    pl.semaphore_signal(barrier, inc=1, device_id={"mdl": other}, device_id_type=pl.DeviceIdType.MESH)
    pl.semaphore_wait(barrier, count)


def gather_kernel(
    count, send, tok, gain, row, wq_hbm, wup_hbm, wdn_hbm,
    recv, hidden, packed, up_pre, part, table,
    msg, wq, wup, wdn, wsem, ssem, rsem, fssem, frsem, tssem, trsem,
):
    me, core = lax.axis_index("tok"), lax.axis_index("mdl")
    other = 1 - core
    bricks, per, width = tok.shape
    slots = recv.shape[1]
    half = per // 2
    mine = pl.ds(pl.multiple_of(core * half, half), half)
    theirs = pl.ds(pl.multiple_of(other * half, half), half)
    loads = [
        pltpu.make_async_copy(a, b, wsem.at[i])
        for i, (a, b) in enumerate(((wq_hbm, wq), (wup_hbm, wup), (wdn_hbm, wdn)))
    ]
    for load in loads:
        load.start()
    greet(me, count, other)

    def out_copy(i):
        peer = lax.rem(me + i + 1, count)
        return remote(msg.at[i], recv.at[me, :, mine, :], ssem.at[i], rsem.at[i], {"tok": peer})

    def launch(i, c):
        peer = lax.rem(me + i + 1, count)
        for k in range(slots):
            msg[i, k] = tok[send[peer * slots + k], mine, :]
        out_copy(i).start()
        return c

    def row_copy(i):
        peer = lax.rem(me + i + 1, count)
        return remote(row, table.at[me], tssem.at[i], trsem.at[i], {"tok": peer})

    def tell(i, c):
        row_copy(i).start()
        return c

    lax.fori_loop(0, count - 1, tell, 0)
    table[me] = row[...]
    lax.fori_loop(0, count - 1, launch, 0)
    for k in range(slots):
        recv[me, k] = tok[send[me * slots + k]]
    x = tok[...].reshape(bricks * per, width).astype(F32)
    inv = lax.rsqrt(jnp.mean(x * x, axis=-1, keepdims=True) + norm_eps)
    hidden[...] = (x * inv * gain[...]).astype(BF16)
    loads[0].wait()
    packed[...] = dot_nn(hidden[...], wq[...]).astype(BF16)
    loads[1].wait()
    loads[2].wait()
    ff = wup.shape[1]
    step = ff // 3
    for n in range(3):
        cols = slice(n * step, (n + 1) * step)
        u = dot_nn(hidden[...], wup[:, cols])
        up_pre[:, cols] = u
        term = dot_nn(gelu_tanh(u).astype(BF16), wdn[cols, :])
        part[...] = term if n == 0 else part[...] + term

    def relay_copy(i, rows):
        source = lax.rem(me - (i + 1) + count, count)
        block = recv.at[source, :, rows, :]
        return remote(block, block, fssem.at[i], frsem.at[i], {"mdl": other})

    def relay(i, c):
        source = lax.rem(me - (i + 1) + count, count)
        remote(msg.at[i], recv.at[source, :, mine, :], ssem.at[i], rsem.at[i], {"tok": source}).wait_recv()
        relay_copy(i, mine).start()
        return c

    lax.fori_loop(0, count - 1, relay, 0)

    def finish(i, c):
        out_copy(i).wait_send()
        row_copy(i).wait_send()
        source = lax.rem(me - (i + 1) + count, count)
        remote(row, table.at[source], tssem.at[i], trsem.at[i], {"tok": source}).wait_recv()
        relay_copy(i, mine).wait_send()
        relay_copy(i, theirs).wait_recv()
        return c

    lax.fori_loop(0, count - 1, finish, 0)


def attend_kernel(
    heads, dh, per, faces, arrival, hidden, packed, recv, gain, wq, bias, seen,
    attended, probs, window, hid, near,
):
    bricks = packed.shape[0] // per
    scale = 1.0 / math.sqrt(dh)
    for b in range(bricks):
        rows = slice(b * per, (b + 1) * per)
        for j in range(faces):
            near[j * per : (j + 1) * per, :] = recv[arrival[b * faces + j]]
        x = near[...].astype(F32)
        inv = lax.rsqrt(jnp.mean(x * x, axis=-1, keepdims=True) + norm_eps)
        h = (x * inv * gain[...]).astype(BF16)
        hid[b, 0:per, :] = hidden[rows, :]
        hid[b, per:, :] = h
        pk = dot_nn(h, wq[...]).astype(BF16)
        for n in range(heads):
            two = slice(n * 2 * dh, (n + 1) * 2 * dh)
            window[b, 0:per, two] = packed[rows, n * 3 * dh + dh : (n + 1) * 3 * dh]
            window[b, per:, two] = pk[:, n * 3 * dh + dh : (n + 1) * 3 * dh]
        live = seen[b : b + 1, :] > 0
        for n in range(heads):
            q = packed[rows, n * 3 * dh : n * 3 * dh + dh]
            k = window[b, :, n * 2 * dh : n * 2 * dh + dh]
            v = window[b, :, n * 2 * dh + dh : (n + 1) * 2 * dh]
            s = dot_nt(q, k) * scale + bias[n]
            s = jnp.where(live, s, -1000000000.0)
            e = jnp.exp(s - jnp.max(s, axis=-1, keepdims=True))
            p = e * (1.0 / jnp.sum(e, axis=-1, keepdims=True))
            probs[b * heads + n] = p
            attended[rows, n * dh : (n + 1) * dh] = dot_nn(p.astype(BF16), v).astype(BF16)


def attend_back_kernel(
    heads, dh, per, faces, arrival, packed, window, hid, probs, mixed, wq,
    own, ret, gw, gp, acc,
):
    bricks = packed.shape[0] // per
    scale = 1.0 / math.sqrt(dh)

    def clear(s, c):
        ret[s] = jnp.zeros(ret.shape[1:], BF16)
        return c

    lax.fori_loop(0, ret.shape[0], clear, 0)
    gp[...] = jnp.zeros(gp.shape, BF16)
    for b in range(bricks):
        rows = slice(b * per, (b + 1) * per)
        for n in range(heads):
            q = packed[rows, n * 3 * dh : n * 3 * dh + dh]
            k = window[b, :, n * 2 * dh : n * 2 * dh + dh]
            v = window[b, :, n * 2 * dh + dh : (n + 1) * 2 * dh]
            p = probs[b * heads + n]
            g = mixed[rows, n * dh : (n + 1) * dh]
            dp = dot_nt(g, v)
            low = (p * (dp - jnp.sum(p * dp, axis=-1, keepdims=True))).astype(BF16)
            at = n * 3 * dh
            gp[0:per, at : at + dh] = (dot_nn(low, k) * scale).astype(BF16)
            gp[:, at + dh : at + 2 * dh] = (dot_tn(low, q) * scale).astype(BF16)
            gp[:, at + 2 * dh : at + 3 * dh] = dot_tn(p.astype(BF16), g).astype(BF16)
        back = dot_nt(gp[...], wq[...])
        own[rows, :] = back[0:per]
        for j in range(faces):
            ret[arrival[b * faces + j]] = back[(j + 1) * per : (j + 2) * per].astype(BF16)
        term = dot_tn(hid[b], gp[...])
        acc[...] = term if b == 0 else acc[...] + term
    gw[...] = acc[...].astype(BF16)


def return_kernel(
    count, send, tok, gain, gout, own, ret, gw, up_pre, wup_hbm, wdn_hbm,
    out, gw_out,
    sib, msg, inbox, part, pmsg, pbox, result, g1a, g1b, s1a, s1b, g2a, g2b, s2, g3, wup, wdn,
    zmsg, zbox, wsem, bs, br, ssem, rsem, xs, xr, zs, zr,
):
    me, core = lax.axis_index("tok"), lax.axis_index("mdl")
    other = 1 - core
    bricks, per, width = tok.shape
    slots = ret.shape[1]
    half = per // 2
    mine = pl.ds(pl.multiple_of(core * half, half), half)
    theirs = pl.ds(pl.multiple_of(other * half, half), half)
    x, y, z = lax.rem(me, 2), lax.rem(me // 2, 2), me // 4
    xn, yn = me + 1 - 2 * x, me + 2 - 4 * y
    loads = [
        pltpu.make_async_copy(a, b, wsem.at[i])
        for i, (a, b) in enumerate(((wup_hbm, wup), (wdn_hbm, wdn)))
    ]
    for load in loads:
        load.start()
    greet(me, count, other)
    cut = gw.shape[-1] // 2

    def plane(q):
        qx, qy = q & 1, q >> 1
        return (1 - y if qy else y) * 2 + (1 - x if qx else x)

    def holder(q, j):
        return lax.rem(z + j, 4) * 4 + plane(q)

    order = (1, 2, 3, 0)

    def sib_copy(q, j):
        i = q * 4 + j
        return remote(ret.at[holder(q, j), :, theirs, :], sib.at[i], bs.at[i], br.at[i], {"mdl": other})

    def give(n, c):
        j = lax.rem(n + 1, 4)
        for q in order:
            sib_copy(q, j).start()
        return c

    lax.fori_loop(0, 4, give, 0)
    one_a = remote(gw.at[:, :, 1 - x, :, pl.ds(0, cut)], g1a, xs.at[0], xr.at[0], {"tok": xn})
    one_b = remote(gw.at[:, 1 - y, :, :, pl.ds(cut, cut)], g1b, xs.at[1], xr.at[1], {"tok": yn})

    def plane_copy(q, j):
        i = q * 4 + j
        return remote(msg.at[i], inbox.at[i], ssem.at[i], rsem.at[i], {"tok": z * 4 + plane(q)})

    def launch(n, c):
        j = lax.rem(n + 1, 4)
        for q in order:
            i = q * 4 + j
            sib_copy(q, j).wait()
            msg[i] = (ret[holder(q, j), :, mine, :].astype(F32) + sib[i].astype(F32)).astype(BF16)
            if q:
                plane_copy(q, j).start()
        return c

    one_a.start()
    one_b.start()
    lax.fori_loop(0, 4, launch, 0)

    for load in loads:
        load.wait()
    ff = wup.shape[1]
    step = ff // 3

    def feed(n):
        cols = slice(n * step, (n + 1) * step)
        act = dot_nt(gout[...], wdn[cols, :])
        pre = (gelu_slope(up_pre[:, cols]) * act).astype(BF16)
        term = dot_nt(pre, wup[:, cols])
        part[...] = part[...] + term

    def merge(j, brick):
        total = jnp.zeros((half, width), F32)
        for q in range(4):
            for k in range(slots):
                i = q * 4 + j
                value = (inbox if q else msg)[i, k].astype(F32)
                named = send[(holder(0, j) * count + z * 4 + plane(q)) * slots + k]
                total = total + jnp.where(named == brick, 1.0, 0.0) * value
        return total

    def z_copy(j):
        return remote(zmsg.at[j - 1], zbox.at[j - 1], zs.at[j - 1], zr.at[j - 1], {"tok": holder(0, j)})

    def pass_on(j):
        for q in (1, 2, 3):
            plane_copy(q, j).wait()

        def one(brick, c):
            zmsg[j - 1, brick] = merge(j, brick).astype(BF16)
            return c

        lax.fori_loop(0, bricks, one, 0)
        z_copy(j).start()

    part[...] = own[...]
    feed(0)
    one_a.wait()
    one_b.wait()
    s1a[...] = (gw[:, :, x, :, 0:cut].astype(F32) + g1a[...].astype(F32)).astype(BF16)
    s1b[...] = (gw[:, y, :, :, cut : 2 * cut].astype(F32) + g1b[...].astype(F32)).astype(BF16)
    two_a = remote(s1a.at[:, 1 - y], g2a, xs.at[2], xr.at[2], {"tok": yn})
    two_b = remote(s1b.at[:, 1 - x], g2b, xs.at[3], xr.at[3], {"tok": xn})
    two_a.start()
    two_b.start()
    pass_on(1)
    feed(1)
    pass_on(2)
    feed(2)
    for b in range(bricks):
        pmsg[b] = part[pl.ds(pl.multiple_of(b * per + other * half, half), half), :].astype(BF16)
    swap_part = remote(pmsg, pbox, xs.at[4], xr.at[4], {"mdl": other})
    swap_part.start()
    pass_on(3)
    two_a.wait()
    two_b.wait()
    s2[:, :, 0:cut] = (s1a[:, y].astype(F32) + g2a[...].astype(F32)).astype(BF16)
    s2[:, :, cut : 2 * cut] = (s1b[:, x].astype(F32) + g2b[...].astype(F32)).astype(BF16)
    last = []
    for d in range(1, 4):
        copy = remote(
            s2.at[lax.rem(z + d, 4)], g3.at[d - 1], xs.at[5 + d], xr.at[5 + d],
            {"tok": lax.rem(me + 4 * d, count)},
        )
        copy.start()
        last.append(copy)
    swap_part.wait()
    for q in (1, 2, 3):
        plane_copy(q, 0).wait()

    def settle(b, c):
        at = pl.ds(pl.multiple_of(b * per + core * half, half), half)
        result[b] = part[at, :] + pbox[b].astype(F32) + merge(0, b)
        return c

    lax.fori_loop(0, bricks, settle, 0)
    for j in range(1, 4):
        z_copy(j).wait()
    result[...] = result[...] + zbox[0].astype(F32) + zbox[1].astype(F32) + zbox[2].astype(F32)
    for b in range(bricks):
        v = tok[b, mine, :].astype(F32)
        inv = lax.rsqrt(jnp.mean(v * v, axis=-1, keepdims=True) + norm_eps)
        normed = v * inv
        g = result[b] * gain[...]
        base = gout[pl.ds(pl.multiple_of(b * per + core * half, half), half), :].astype(F32)
        out[b, mine, :] = (
            base + inv * (g - normed * jnp.mean(g * normed, axis=-1, keepdims=True))
        ).astype(BF16)
    share = remote(out.at[:, mine, :], out.at[:, mine, :], xs.at[5], xr.at[5], {"mdl": other})
    share.start()
    for copy in last:
        copy.wait()
    gw_out[...] = (
        s2[z].astype(F32) + g3[0].astype(F32) + g3[1].astype(F32) + g3[2].astype(F32)
    )
    share.wait_send()
    remote(out.at[:, theirs, :], out.at[:, theirs, :], xs.at[5], xr.at[5], {"mdl": other}).wait_recv()


def body(
    tokens,
    cotangent,
    norm_gain,
    w_qkv,
    w_out,
    w_up,
    w_down,
    w_disp,
    rel_bias,
    face_source,
    face_live,
    send_bricks,
):
    bricks, per, width = tokens.shape
    rows = bricks * per
    heads = rel_bias.shape[0]
    dh = w_out.shape[0] // heads
    faces = face_source.shape[1]
    devices = lax.axis_size("tok")
    slots = send_bricks.shape[2]
    total = devices * slots
    kv = heads * 2 * dh
    wide = heads * 3 * dh
    span = (faces + 1) * per
    ff = w_up.shape[1]
    half = per // 2
    send = send_bricks.reshape(-1)
    row = jnp.zeros((8, 128), jnp.int32).at[0, : devices * slots].set(send)
    sources = face_source.reshape(-1)
    matches = (sources[:, None] == sources[None, :]).astype(jnp.int32)
    count = sources.shape[0]
    before = jnp.arange(count)[None, :] < jnp.arange(count)[:, None]
    arrival = sources * slots + jnp.sum(jnp.where(before, matches, 0), axis=1)
    seen = jnp.concatenate([jnp.ones((bricks, 1), jnp.int32), face_live], axis=1)
    seen = jnp.repeat(seen, per, axis=1)
    gain = norm_gain.reshape(1, width)
    flat = tokens.reshape(rows, width)
    any_spec = pl.BlockSpec(memory_space=pl.ANY)
    dma = pltpu.SemaphoreType.DMA

    def shape(dims, kind=BF16):
        return jax.ShapeDtypeStruct(dims, kind)

    def talk(ident):
        return pltpu.CompilerParams(
            vmem_limit_bytes=48 << 20, collective_id=ident, has_side_effects=True
        )

    recv, hidden, packed, up_pre, part_ffn, table = pl.pallas_call(
        functools.partial(gather_kernel, devices),
        out_shape=(
            shape((devices, slots, per, width)),
            shape((rows, width)),
            shape((rows, wide)),
            shape((rows, ff), F32),
            shape((rows, width), F32),
            shape((devices, 8, 128), jnp.int32),
        ),
        in_specs=[SM, VM, VM, VM, any_spec, any_spec, any_spec],
        out_specs=(VM,) * 6,
        scratch_shapes=[
            pltpu.VMEM((devices - 1, slots, half, width), BF16),
            pltpu.VMEM((width, wide), BF16),
            pltpu.VMEM((width, ff), BF16),
            pltpu.VMEM((ff, width), BF16),
            dma((3,)),
            dma((devices - 1,)),
            dma((devices - 1,)),
            dma((devices - 1,)),
            dma((devices - 1,)),
            dma((devices - 1,)),
            dma((devices - 1,)),
        ],
        compiler_params=talk(2),
        name="gather",
    )(send, tokens, gain, row, w_qkv, w_up, w_down)

    attended, probs, window, hid = pl.pallas_call(
        functools.partial(attend_kernel, heads, dh, per, faces),
        out_shape=(
            shape((rows, heads * dh)),
            shape((bricks * heads, per, span), F32),
            shape((bricks, span, kv)),
            shape((bricks, span, width)),
        ),
        in_specs=[SM] + [VM] * 7,
        out_specs=(VM,) * 4,
        scratch_shapes=[pltpu.VMEM((faces * per, width), BF16)],
        compiler_params=PARAMS,
        name="attend",
    )(arrival, hidden, packed, recv.reshape(total, per, width), gain, w_qkv, rel_bias, seen)

    part_out = part_ffn + jnp.dot(attended, w_out, preferred_element_type=F32)
    folding, grad_out = pl.pallas_call(
        fold_swap_kernel,
        out_shape=(shape((1, rows), F32), shape((rows, width))),
        in_specs=[VM] * 4,
        out_specs=(VM, VM),
        scratch_shapes=[pltpu.VMEM((rows, width), F32), dma, dma],
        compiler_params=talk(0),
        name="fold_swap",
    )(flat, part_out, cotangent.reshape(rows, width), w_disp)
    grad_mixed = jnp.dot(grad_out, w_out.T, preferred_element_type=F32).astype(BF16)

    own, ret, gw = pl.pallas_call(
        functools.partial(attend_back_kernel, heads, dh, per, faces),
        out_shape=(
            shape((rows, width), F32),
            shape((total, per, width)),
            shape((width, wide)),
        ),
        in_specs=[SM] + [VM] * 6,
        out_specs=(VM,) * 3,
        scratch_shapes=[pltpu.VMEM((span, wide), BF16), pltpu.VMEM((width, wide), F32)],
        compiler_params=PARAMS,
        name="attend_back",
    )(arrival, packed, window, hid, probs, grad_mixed, w_qkv)

    piece = width // devices
    cut = wide // 2
    grad_tokens, grad_weight = pl.pallas_call(
        functools.partial(return_kernel, devices),
        out_shape=(shape((bricks, per, width)), shape((piece, wide), F32)),
        in_specs=[SM] + [VM] * 7 + [any_spec] * 2,
        out_specs=(VM, VM),
        scratch_shapes=[
            pltpu.VMEM((devices, slots, half, width), BF16),
            pltpu.VMEM((devices, slots, half, width), BF16),
            pltpu.VMEM((devices, slots, half, width), BF16),
            pltpu.VMEM((rows, width), F32),
            pltpu.VMEM((bricks, half, width), BF16),
            pltpu.VMEM((bricks, half, width), BF16),
            pltpu.VMEM((bricks, half, width), F32),
            pltpu.VMEM((4, 2, piece, cut), BF16),
            pltpu.VMEM((4, 2, piece, cut), BF16),
            pltpu.VMEM((4, 2, piece, cut), BF16),
            pltpu.VMEM((4, 2, piece, cut), BF16),
            pltpu.VMEM((4, piece, cut), BF16),
            pltpu.VMEM((4, piece, cut), BF16),
            pltpu.VMEM((4, piece, wide), BF16),
            pltpu.VMEM((3, piece, wide), BF16),
            pltpu.VMEM((width, ff), BF16),
            pltpu.VMEM((ff, width), BF16),
            pltpu.VMEM((3, bricks, half, width), BF16),
            pltpu.VMEM((3, bricks, half, width), BF16),
            dma((2,)),
            dma((devices,)),
            dma((devices,)),
            dma((devices,)),
            dma((devices,)),
            dma((9,)),
            dma((9,)),
            dma((3,)),
            dma((3,)),
        ],
        compiler_params=talk(1),
        name="give_back",
    )(
        table[:, 0, : devices * slots].reshape(-1),
        tokens,
        gain,
        grad_out,
        own,
        ret.reshape(devices, slots, per, width),
        gw.reshape(4, 2, 2, piece, wide),
        up_pre,
        w_up,
        w_down,
    )
    return (folding.reshape(bricks, per), grad_tokens, grad_weight)


def solution(mesh):
    return jax.shard_map(
        body if mesh.shape["tok"] == 16 and mesh.shape["mdl"] == 2 else body_wide,
        mesh=mesh,
        in_specs=(
            P("tok", None, None),
            P("tok", None, None),
            P(),
            P(None, "mdl"),
            P("mdl", None),
            P(None, "mdl"),
            P("mdl", None),
            P(),
            P("mdl", None, None),
            P("tok", None),
            P("tok", None),
            P("tok", None, None),
        ),
        out_specs=(P("tok", None), P("tok", None, None), P("tok", "mdl")),
        check_vma=False,
    )
```

```python
import functools
import math

import jax
import jax.numpy as jnp
from jax import lax
from jax.experimental import pallas as pl
from jax.experimental.pallas import tpu as pltpu
from jax.sharding import PartitionSpec as P

fold_weight = 8.0
norm_eps = 1e-05
F32 = jnp.float32
BF16 = jnp.bfloat16
VM = pl.BlockSpec(memory_space=pltpu.VMEM)
SM = pl.BlockSpec(memory_space=pltpu.SMEM)
PARAMS = pltpu.CompilerParams(vmem_limit_bytes=40 << 20)


def dot_nn(a, b):
    return lax.dot_general(a, b, (((1,), (0,)), ((), ())), preferred_element_type=F32)


def dot_nt(a, b):
    return lax.dot_general(a, b, (((1,), (1,)), ((), ())), preferred_element_type=F32)


def dot_tn(a, b):
    return lax.dot_general(a, b, (((0,), (0,)), ((), ())), preferred_element_type=F32)


def gelu_tanh(value):
    return jax.nn.gelu(value, approximate=True)


def project_kernel(heads, dh, send, tok, gain, w, hidden, packed, outgoing, pairs):
    bricks, per, width = tok.shape
    x = tok[...].reshape(bricks * per, width).astype(F32)
    inv = lax.rsqrt(jnp.mean(x * x, axis=-1, keepdims=True) + norm_eps)
    h = (x * inv * gain[...]).astype(BF16)
    hidden[...] = h
    pk = dot_nn(h, w[...]).astype(BF16)
    packed[...] = pk
    for b in range(bricks):
        for n in range(heads):
            pairs[b, :, n * 2 * dh : (n + 1) * 2 * dh] = pk[
                b * per : (b + 1) * per, n * 3 * dh + dh : (n + 1) * 3 * dh
            ]

    def put(s, c):
        outgoing[s] = pairs[send[s]]
        return c

    lax.fori_loop(0, outgoing.shape[0], put, 0)


def fill_window(arrival, packed, incoming, window, b, heads, dh, per, faces):
    for n in range(heads):
        window[0:per, n * 2 * dh : (n + 1) * 2 * dh] = packed[
            b * per : (b + 1) * per, n * 3 * dh + dh : (n + 1) * 3 * dh
        ]
    for j in range(faces):
        window[(j + 1) * per : (j + 2) * per, :] = incoming[arrival[b * faces + j]]


def forward_kernel(heads, dh, per, faces, arrival, packed, incoming, bias, seen, attended, probs, window):
    bricks = packed.shape[0] // per
    scale = 1.0 / math.sqrt(dh)
    for b in range(bricks):
        fill_window(arrival, packed, incoming, window, b, heads, dh, per, faces)
        live = seen[b : b + 1, :] > 0
        rows = slice(b * per, (b + 1) * per)
        for n in range(heads):
            q = packed[rows, n * 3 * dh : n * 3 * dh + dh]
            k = window[:, n * 2 * dh : n * 2 * dh + dh]
            v = window[:, n * 2 * dh + dh : (n + 1) * 2 * dh]
            s = dot_nt(q, k) * scale + bias[n]
            s = jnp.where(live, s, -1000000000.0)
            e = jnp.exp(s - jnp.max(s, axis=-1, keepdims=True))
            p = e * (1.0 / jnp.sum(e, axis=-1, keepdims=True))
            probs[b * heads + n] = p
            attended[rows, n * dh : (n + 1) * dh] = dot_nn(p.astype(BF16), v).astype(BF16)


def backward_kernel(
    heads, dh, per, faces, arrival, packed, incoming, probs, mixed, gquery, gown, returning, window, gwin
):
    bricks = packed.shape[0] // per
    scale = 1.0 / math.sqrt(dh)

    def clear(s, c):
        returning[s] = jnp.zeros(returning.shape[1:], BF16)
        return c

    lax.fori_loop(0, returning.shape[0], clear, 0)
    for b in range(bricks):
        fill_window(arrival, packed, incoming, window, b, heads, dh, per, faces)
        rows = slice(b * per, (b + 1) * per)
        for n in range(heads):
            q = packed[rows, n * 3 * dh : n * 3 * dh + dh]
            k = window[:, n * 2 * dh : n * 2 * dh + dh]
            v = window[:, n * 2 * dh + dh : (n + 1) * 2 * dh]
            p = probs[b * heads + n]
            g = mixed[rows, n * dh : (n + 1) * dh]
            dp = dot_nt(g, v)
            ds = p * (dp - jnp.sum(p * dp, axis=-1, keepdims=True))
            low = ds.astype(BF16)
            gquery[rows, n * dh : (n + 1) * dh] = dot_nn(low, k) * scale
            gwin[:, n * 2 * dh : n * 2 * dh + dh] = dot_tn(low, q) * scale
            gwin[:, n * 2 * dh + dh : (n + 1) * 2 * dh] = dot_tn(p.astype(BF16), g)
        gown[b] = gwin[0:per, :]
        for j in range(faces):
            returning[arrival[b * faces + j]] = gwin[(j + 1) * per : (j + 2) * per, :].astype(BF16)


def collect_kernel(heads, dh, send, returned, gquery, gown, gpacked, acc):
    bricks, per, _ = gown.shape
    acc[...] = gown[...]

    def add(s, c):
        acc[send[s]] += returned[s].astype(F32)
        return c

    lax.fori_loop(0, returned.shape[0], add, 0)
    for b in range(bricks):
        rows = slice(b * per, (b + 1) * per)
        for n in range(heads):
            gpacked[rows, n * 3 * dh : n * 3 * dh + dh] = gquery[rows, n * dh : (n + 1) * dh].astype(BF16)
            gpacked[rows, n * 3 * dh + dh : (n + 1) * 3 * dh] = acc[
                b, :, n * 2 * dh : (n + 1) * 2 * dh
            ].astype(BF16)


def swap(src, dst, send_sem, recv_sem):
    other = 1 - lax.axis_index("mdl")
    barrier = pltpu.get_barrier_semaphore()
    pl.semaphore_signal(barrier, inc=1, device_id={"mdl": other}, device_id_type=pl.DeviceIdType.MESH)
    pl.semaphore_wait(barrier, 1)
    copy = pltpu.make_async_remote_copy(
        src_ref=src,
        dst_ref=dst,
        send_sem=send_sem,
        recv_sem=recv_sem,
        device_id={"mdl": other},
        device_id_type=pl.DeviceIdType.MESH,
    )
    copy.start()
    return copy


def fold_math(x, total, cot, w_disp, folding, grad_out):
    out = (x.astype(F32) + total).astype(BF16)
    disp = lax.dot_general(w_disp, out, (((0,), (1,)), ((), ())), preferred_element_type=F32)
    vox = disp.shape[0] // 3
    steps = (1, 4, 16)
    comp = [disp[c * vox : (c + 1) * vox] for c in range(3)]
    row = lax.broadcasted_iota(jnp.int32, comp[0].shape, 0)
    inside = ((row & 3) < 3) & (((row >> 2) & 3) < 3) & ((row >> 4) < 3)
    jac = [
        [
            pltpu.roll(comp[i], vox - steps[k], 0) - comp[i] + (1.0 if i == k else 0.0)
            for k in range(3)
        ]
        for i in range(3)
    ]
    cof = [[None] * 3 for _ in range(3)]
    for i in range(3):
        i1, i2 = (i + 1) % 3, (i + 2) % 3
        for k in range(3):
            k1, k2 = (k + 1) % 3, (k + 2) % 3
            cof[i][k] = jac[i1][k1] * jac[i2][k2] - jac[i1][k2] * jac[i2][k1]
    det = jac[0][0] * cof[0][0] + jac[0][1] * cof[0][1] + jac[0][2] * cof[0][2]
    small = jnp.exp(-jnp.abs(det))
    soft = jnp.maximum(-det, 0.0) + jnp.log1p(small)
    folding[...] = jnp.sum(jnp.where(inside, soft, 0.0), axis=0, keepdims=True) * (1.0 / 27.0)
    sig = jnp.where(det > 0, small, 1.0) / (1.0 + small)
    coef = jnp.where(inside, sig * (-fold_weight / 27.0), 0.0)
    grads = []
    for i in range(3):
        g = jnp.zeros_like(det)
        for k in range(3):
            t = jnp.where(inside, coef * cof[i][k], 0.0)
            g = g + pltpu.roll(t, steps[k], 0) - t
        grads.append(g)
    gd = jnp.concatenate(grads, axis=0).astype(BF16)
    back = lax.dot_general(gd, w_disp, (((0,), (1,)), ((), ())), preferred_element_type=F32)
    grad_out[...] = (cot.astype(F32) + back).astype(BF16)


def fold_swap_kernel(x, part, cot, w_disp, folding, grad_out, other, send_sem, recv_sem):
    swap(part, other, send_sem, recv_sem).wait()
    fold_math(x[...], part[...] + other[...], cot[...], w_disp[...], folding, grad_out)


def fold_kernel(x, part, cot, w_disp, folding, grad_out):
    fold_math(x[...], part[...], cot[...], w_disp[...], folding, grad_out)


def norm_math(x, grad_hidden, grad_out, gain, out):
    x = x.astype(F32)
    inv = lax.rsqrt(jnp.mean(x * x, axis=-1, keepdims=True) + norm_eps)
    normed = x * inv
    g = grad_hidden * gain
    out[...] = (
        grad_out.astype(F32) + inv * (g - normed * jnp.mean(g * normed, axis=-1, keepdims=True))
    ).astype(BF16)


def norm_swap_kernel(x, part, grad_out, gain, out, other, send_sem, recv_sem):
    swap(part, other, send_sem, recv_sem).wait()
    norm_math(x[...], part[...].astype(F32) + other[...].astype(F32), grad_out[...], gain[...], out)


def norm_kernel(x, part, grad_out, gain, out):
    norm_math(x[...], part[...].astype(F32), grad_out[...], gain[...], out)


def body_wide(
    tokens,
    cotangent,
    norm_gain,
    w_qkv,
    w_out,
    w_up,
    w_down,
    w_disp,
    rel_bias,
    face_source,
    face_live,
    send_bricks,
):
    bricks, per, width = tokens.shape
    rows = bricks * per
    heads = rel_bias.shape[0]
    dh = w_out.shape[0] // heads
    faces = face_source.shape[1]
    devices = lax.axis_size("tok")
    pair = lax.axis_size("mdl") == 2
    slots = send_bricks.shape[2]
    total = devices * slots
    kv = heads * 2 * dh
    span = (faces + 1) * per
    send = send_bricks.reshape(-1)
    sources = face_source.reshape(-1)
    matches = (sources[:, None] == sources[None, :]).astype(jnp.int32)
    count = sources.shape[0]
    before = jnp.arange(count)[None, :] < jnp.arange(count)[:, None]
    arrival = sources * slots + jnp.sum(jnp.where(before, matches, 0), axis=1)
    seen = jnp.concatenate([jnp.ones((bricks, 1), jnp.int32), face_live], axis=1)
    seen = jnp.repeat(seen, per, axis=1)
    gain = norm_gain.reshape(1, width)
    flat = tokens.reshape(rows, width)

    hidden, packed, outgoing = pl.pallas_call(
        functools.partial(project_kernel, heads, dh),
        out_shape=(
            jax.ShapeDtypeStruct((rows, width), BF16),
            jax.ShapeDtypeStruct((rows, heads * 3 * dh), BF16),
            jax.ShapeDtypeStruct((total, per, kv), BF16),
        ),
        in_specs=[SM, VM, VM, VM],
        out_specs=(VM, VM, VM),
        scratch_shapes=[pltpu.VMEM((bricks, per, kv), BF16)],
        compiler_params=PARAMS,
        name="project",
    )(send, tokens, gain, w_qkv)

    incoming = lax.all_to_all(outgoing, "tok", split_axis=0, concat_axis=0, tiled=True)

    up_pre = jnp.dot(hidden, w_up, preferred_element_type=F32)
    activ, gelu_back = jax.vjp(gelu_tanh, up_pre)
    part_ffn = jnp.dot(activ.astype(BF16), w_down, preferred_element_type=F32)

    attended, probs = pl.pallas_call(
        functools.partial(forward_kernel, heads, dh, per, faces),
        out_shape=(
            jax.ShapeDtypeStruct((rows, heads * dh), BF16),
            jax.ShapeDtypeStruct((bricks * heads, per, span), F32),
        ),
        in_specs=[SM, VM, VM, VM, VM],
        out_specs=(VM, VM),
        scratch_shapes=[pltpu.VMEM((span, kv), BF16)],
        compiler_params=PARAMS,
        name="attend",
    )(arrival, packed, incoming, rel_bias, seen)

    part_out = part_ffn + jnp.dot(attended, w_out, preferred_element_type=F32)
    fold_shape = (
        jax.ShapeDtypeStruct((1, rows), F32),
        jax.ShapeDtypeStruct((rows, width), BF16),
    )
    cot = cotangent.reshape(rows, width)
    if pair:
        folding, grad_out = pl.pallas_call(
            fold_swap_kernel,
            out_shape=fold_shape,
            in_specs=[VM] * 4,
            out_specs=(VM, VM),
            scratch_shapes=[
                pltpu.VMEM((rows, width), F32),
                pltpu.SemaphoreType.DMA,
                pltpu.SemaphoreType.DMA,
            ],
            compiler_params=pltpu.CompilerParams(
                vmem_limit_bytes=40 << 20, collective_id=0, has_side_effects=True
            ),
            name="fold_swap",
        )(flat, part_out, cot, w_disp)
    else:
        folding, grad_out = pl.pallas_call(
            fold_kernel,
            out_shape=fold_shape,
            in_specs=[VM] * 4,
            out_specs=(VM, VM),
            compiler_params=PARAMS,
            name="fold",
        )(flat, lax.psum(part_out, "mdl"), cot, w_disp)

    grad_mixed = jnp.dot(grad_out, w_out.T, preferred_element_type=F32).astype(BF16)

    gquery, gown, returning = pl.pallas_call(
        functools.partial(backward_kernel, heads, dh, per, faces),
        out_shape=(
            jax.ShapeDtypeStruct((rows, heads * dh), F32),
            jax.ShapeDtypeStruct((bricks, per, kv), F32),
            jax.ShapeDtypeStruct((total, per, kv), BF16),
        ),
        in_specs=[SM, VM, VM, VM, VM],
        out_specs=(VM, VM, VM),
        scratch_shapes=[pltpu.VMEM((span, kv), BF16), pltpu.VMEM((span, kv), F32)],
        compiler_params=PARAMS,
        name="attend_back",
    )(arrival, packed, incoming, probs, grad_mixed)

    returned = lax.all_to_all(returning, "tok", split_axis=0, concat_axis=0, tiled=True)

    grad_act = jnp.dot(grad_out, w_down.T, preferred_element_type=F32)
    grad_pre = gelu_back(grad_act)[0].astype(BF16)
    part_up = jnp.dot(grad_pre, w_up.T, preferred_element_type=F32)

    grad_packed = pl.pallas_call(
        functools.partial(collect_kernel, heads, dh),
        out_shape=jax.ShapeDtypeStruct((rows, heads * 3 * dh), BF16),
        in_specs=[SM, VM, VM, VM],
        out_specs=VM,
        scratch_shapes=[pltpu.VMEM((bricks, per, kv), F32)],
        compiler_params=PARAMS,
        name="collect",
    )(send, returned, gquery, gown)

    terms = lax.dot_general(
        hidden, grad_packed, (((0,), (0,)), ((), ())), preferred_element_type=F32
    ).astype(BF16)
    terms = terms.reshape(devices, width // devices, heads * 3 * dh)
    terms = lax.all_to_all(terms, "tok", split_axis=0, concat_axis=0, tiled=True)
    grad_weight = jnp.sum(terms.astype(F32), axis=0)

    grad_part = (part_up + jnp.dot(grad_packed, w_qkv.T, preferred_element_type=F32)).astype(BF16)
    norm_shape = jax.ShapeDtypeStruct((rows, width), BF16)
    if pair:
        grad_tokens = pl.pallas_call(
            norm_swap_kernel,
            out_shape=norm_shape,
            in_specs=[VM] * 4,
            out_specs=VM,
            scratch_shapes=[
                pltpu.VMEM((rows, width), BF16),
                pltpu.SemaphoreType.DMA,
                pltpu.SemaphoreType.DMA,
            ],
            compiler_params=pltpu.CompilerParams(
                vmem_limit_bytes=40 << 20, collective_id=1, has_side_effects=True
            ),
            name="norm_swap",
        )(flat, grad_part, grad_out, gain)
    else:
        grad_tokens = pl.pallas_call(
            norm_kernel,
            out_shape=norm_shape,
            in_specs=[VM] * 4,
            out_specs=VM,
            compiler_params=PARAMS,
            name="norm",
        )(flat, lax.psum(grad_part, "mdl"), grad_out, gain)
    return (folding.reshape(bricks, per), grad_tokens.reshape(bricks, per, width), grad_weight)


def gelu_slope(u):
    c = math.sqrt(2.0 / math.pi)
    t = jnp.tanh(c * (u + 0.044715 * (u * u * u)))
    return 0.5 * (1.0 + t) + 0.5 * u * (1.0 - t * t) * c * (1.0 + (3.0 * 0.044715) * (u * u))


def remote(src, dst, send_sem, recv_sem, where):
    return pltpu.make_async_remote_copy(
        src_ref=src,
        dst_ref=dst,
        send_sem=send_sem,
        recv_sem=recv_sem,
        device_id=where,
        device_id_type=pl.DeviceIdType.MESH,
    )


def greet(me, count, other):
    barrier = pltpu.get_barrier_semaphore()

    def hail(i, c):
        peer = lax.rem(me + i + 1, count)
        pl.semaphore_signal(barrier, inc=1, device_id={"tok": peer}, device_id_type=pl.DeviceIdType.MESH)
        return c

    lax.fori_loop(0, count - 1, hail, 0)
    pl.semaphore_signal(barrier, inc=1, device_id={"mdl": other}, device_id_type=pl.DeviceIdType.MESH)
    pl.semaphore_wait(barrier, count)


def gather_kernel(
    count, send, tok, gain, row, wq_hbm, wup_hbm, wdn_hbm,
    recv, hidden, packed, up_pre, part, table,
    msg, wq, wup, wdn, wsem, ssem, rsem, fssem, frsem, tssem, trsem,
):
    me, core = lax.axis_index("tok"), lax.axis_index("mdl")
    other = 1 - core
    bricks, per, width = tok.shape
    slots = recv.shape[1]
    half = per // 2
    mine = pl.ds(pl.multiple_of(core * half, half), half)
    theirs = pl.ds(pl.multiple_of(other * half, half), half)
    loads = [
        pltpu.make_async_copy(a, b, wsem.at[i])
        for i, (a, b) in enumerate(((wq_hbm, wq), (wup_hbm, wup), (wdn_hbm, wdn)))
    ]
    for load in loads:
        load.start()
    greet(me, count, other)

    def out_copy(i):
        peer = lax.rem(me + i + 1, count)
        return remote(msg.at[i], recv.at[me, :, mine, :], ssem.at[i], rsem.at[i], {"tok": peer})

    def launch(i, c):
        peer = lax.rem(me + i + 1, count)
        for k in range(slots):
            msg[i, k] = tok[send[peer * slots + k], mine, :]
        out_copy(i).start()
        return c

    def row_copy(i):
        peer = lax.rem(me + i + 1, count)
        return remote(row, table.at[me], tssem.at[i], trsem.at[i], {"tok": peer})

    def tell(i, c):
        row_copy(i).start()
        return c

    lax.fori_loop(0, count - 1, tell, 0)
    table[me] = row[...]
    lax.fori_loop(0, count - 1, launch, 0)
    for k in range(slots):
        recv[me, k] = tok[send[me * slots + k]]
    x = tok[...].reshape(bricks * per, width).astype(F32)
    inv = lax.rsqrt(jnp.mean(x * x, axis=-1, keepdims=True) + norm_eps)
    hidden[...] = (x * inv * gain[...]).astype(BF16)
    loads[0].wait()
    packed[...] = dot_nn(hidden[...], wq[...]).astype(BF16)
    loads[1].wait()
    loads[2].wait()
    ff = wup.shape[1]
    step = ff // 3
    for n in range(3):
        cols = slice(n * step, (n + 1) * step)
        u = dot_nn(hidden[...], wup[:, cols])
        up_pre[:, cols] = u
        term = dot_nn(gelu_tanh(u).astype(BF16), wdn[cols, :])
        part[...] = term if n == 0 else part[...] + term

    def relay_copy(i, rows):
        source = lax.rem(me - (i + 1) + count, count)
        block = recv.at[source, :, rows, :]
        return remote(block, block, fssem.at[i], frsem.at[i], {"mdl": other})

    def relay(i, c):
        source = lax.rem(me - (i + 1) + count, count)
        remote(msg.at[i], recv.at[source, :, mine, :], ssem.at[i], rsem.at[i], {"tok": source}).wait_recv()
        relay_copy(i, mine).start()
        return c

    lax.fori_loop(0, count - 1, relay, 0)

    def finish(i, c):
        out_copy(i).wait_send()
        row_copy(i).wait_send()
        source = lax.rem(me - (i + 1) + count, count)
        remote(row, table.at[source], tssem.at[i], trsem.at[i], {"tok": source}).wait_recv()
        relay_copy(i, mine).wait_send()
        relay_copy(i, theirs).wait_recv()
        return c

    lax.fori_loop(0, count - 1, finish, 0)


def attend_kernel(
    heads, dh, per, faces, arrival, hidden, packed, recv, gain, wq, bias, seen,
    attended, probs, window, hid, near,
):
    bricks = packed.shape[0] // per
    scale = 1.0 / math.sqrt(dh)
    for b in range(bricks):
        rows = slice(b * per, (b + 1) * per)
        for j in range(faces):
            near[j * per : (j + 1) * per, :] = recv[arrival[b * faces + j]]
        x = near[...].astype(F32)
        inv = lax.rsqrt(jnp.mean(x * x, axis=-1, keepdims=True) + norm_eps)
        h = (x * inv * gain[...]).astype(BF16)
        hid[b, 0:per, :] = hidden[rows, :]
        hid[b, per:, :] = h
        pk = dot_nn(h, wq[...]).astype(BF16)
        for n in range(heads):
            two = slice(n * 2 * dh, (n + 1) * 2 * dh)
            window[b, 0:per, two] = packed[rows, n * 3 * dh + dh : (n + 1) * 3 * dh]
            window[b, per:, two] = pk[:, n * 3 * dh + dh : (n + 1) * 3 * dh]
        live = seen[b : b + 1, :] > 0
        for n in range(heads):
            q = packed[rows, n * 3 * dh : n * 3 * dh + dh]
            k = window[b, :, n * 2 * dh : n * 2 * dh + dh]
            v = window[b, :, n * 2 * dh + dh : (n + 1) * 2 * dh]
            s = dot_nt(q, k) * scale + bias[n]
            s = jnp.where(live, s, -1000000000.0)
            e = jnp.exp(s - jnp.max(s, axis=-1, keepdims=True))
            p = e * (1.0 / jnp.sum(e, axis=-1, keepdims=True))
            probs[b * heads + n] = p
            attended[rows, n * dh : (n + 1) * dh] = dot_nn(p.astype(BF16), v).astype(BF16)


def attend_back_kernel(
    heads, dh, per, faces, arrival, packed, window, hid, probs, mixed, wq,
    own, ret, gw, gp, acc,
):
    bricks = packed.shape[0] // per
    scale = 1.0 / math.sqrt(dh)

    def clear(s, c):
        ret[s] = jnp.zeros(ret.shape[1:], BF16)
        return c

    lax.fori_loop(0, ret.shape[0], clear, 0)
    gp[...] = jnp.zeros(gp.shape, BF16)
    for b in range(bricks):
        rows = slice(b * per, (b + 1) * per)
        for n in range(heads):
            q = packed[rows, n * 3 * dh : n * 3 * dh + dh]
            k = window[b, :, n * 2 * dh : n * 2 * dh + dh]
            v = window[b, :, n * 2 * dh + dh : (n + 1) * 2 * dh]
            p = probs[b * heads + n]
            g = mixed[rows, n * dh : (n + 1) * dh]
            dp = dot_nt(g, v)
            low = (p * (dp - jnp.sum(p * dp, axis=-1, keepdims=True))).astype(BF16)
            at = n * 3 * dh
            gp[0:per, at : at + dh] = (dot_nn(low, k) * scale).astype(BF16)
            gp[:, at + dh : at + 2 * dh] = (dot_tn(low, q) * scale).astype(BF16)
            gp[:, at + 2 * dh : at + 3 * dh] = dot_tn(p.astype(BF16), g).astype(BF16)
        back = dot_nt(gp[...], wq[...])
        own[rows, :] = back[0:per]
        for j in range(faces):
            ret[arrival[b * faces + j]] = back[(j + 1) * per : (j + 2) * per].astype(BF16)
        term = dot_tn(hid[b], gp[...])
        acc[...] = term if b == 0 else acc[...] + term
    gw[...] = acc[...].astype(BF16)


def return_kernel(
    count, send, tok, gain, gout, own, ret, gw, up_pre, wup_hbm, wdn_hbm,
    out, gw_out,
    sib, msg, inbox, part, pmsg, pbox, result, g1a, g1b, s1a, s1b, g2a, g2b, s2, g3, wup, wdn,
    zmsg, zbox, wsem, bs, br, ssem, rsem, xs, xr, zs, zr,
):
    me, core = lax.axis_index("tok"), lax.axis_index("mdl")
    other = 1 - core
    bricks, per, width = tok.shape
    slots = ret.shape[1]
    half = per // 2
    mine = pl.ds(pl.multiple_of(core * half, half), half)
    theirs = pl.ds(pl.multiple_of(other * half, half), half)
    x, y, z = lax.rem(me, 2), lax.rem(me // 2, 2), me // 4
    xn, yn = me + 1 - 2 * x, me + 2 - 4 * y
    loads = [
        pltpu.make_async_copy(a, b, wsem.at[i])
        for i, (a, b) in enumerate(((wup_hbm, wup), (wdn_hbm, wdn)))
    ]
    for load in loads:
        load.start()
    greet(me, count, other)
    cut = gw.shape[-1] // 2

    def plane(q):
        qx, qy = q & 1, q >> 1
        return (1 - y if qy else y) * 2 + (1 - x if qx else x)

    def holder(q, j):
        return lax.rem(z + j, 4) * 4 + plane(q)

    order = (1, 2, 3, 0)

    def sib_copy(q, j):
        i = q * 4 + j
        return remote(ret.at[holder(q, j), :, theirs, :], sib.at[i], bs.at[i], br.at[i], {"mdl": other})

    def give(n, c):
        j = lax.rem(n + 1, 4)
        for q in order:
            sib_copy(q, j).start()
        return c

    lax.fori_loop(0, 4, give, 0)
    one_a = remote(gw.at[:, :, 1 - x, :, pl.ds(0, cut)], g1a, xs.at[0], xr.at[0], {"tok": xn})
    one_b = remote(gw.at[:, 1 - y, :, :, pl.ds(cut, cut)], g1b, xs.at[1], xr.at[1], {"tok": yn})

    def plane_copy(q, j):
        i = q * 4 + j
        return remote(msg.at[i], inbox.at[i], ssem.at[i], rsem.at[i], {"tok": z * 4 + plane(q)})

    def launch(n, c):
        j = lax.rem(n + 1, 4)
        for q in order:
            i = q * 4 + j
            sib_copy(q, j).wait()
            msg[i] = (ret[holder(q, j), :, mine, :].astype(F32) + sib[i].astype(F32)).astype(BF16)
            if q:
                plane_copy(q, j).start()
        return c

    one_a.start()
    one_b.start()
    lax.fori_loop(0, 2, launch, 0)

    for load in loads:
        load.wait()
    ff = wup.shape[1]
    step = ff // 3

    def feed(n):
        cols = slice(n * step, (n + 1) * step)
        act = dot_nt(gout[...], wdn[cols, :])
        pre = (gelu_slope(up_pre[:, cols]) * act).astype(BF16)
        term = dot_nt(pre, wup[:, cols])
        part[...] = part[...] + term

    def merge(j, brick):
        total = jnp.zeros((half, width), F32)
        for q in range(4):
            for k in range(slots):
                i = q * 4 + j
                value = (inbox if q else msg)[i, k].astype(F32)
                named = send[(holder(0, j) * count + z * 4 + plane(q)) * slots + k]
                total = total + jnp.where(named == brick, 1.0, 0.0) * value
        return total

    def z_copy(j):
        return remote(zmsg.at[j - 1], zbox.at[j - 1], zs.at[j - 1], zr.at[j - 1], {"tok": holder(0, j)})

    def pass_on(j):
        for q in (1, 2, 3):
            plane_copy(q, j).wait()

        def one(brick, c):
            zmsg[j - 1, brick] = merge(j, brick).astype(BF16)
            return c

        lax.fori_loop(0, bricks, one, 0)
        z_copy(j).start()

    part[...] = own[...]
    feed(0)
    one_a.wait()
    one_b.wait()
    s1a[...] = (gw[:, :, x, :, 0:cut].astype(F32) + g1a[...].astype(F32)).astype(BF16)
    s1b[...] = (gw[:, y, :, :, cut : 2 * cut].astype(F32) + g1b[...].astype(F32)).astype(BF16)
    two_a = remote(s1a.at[:, 1 - y], g2a, xs.at[2], xr.at[2], {"tok": yn})
    two_b = remote(s1b.at[:, 1 - x], g2b, xs.at[3], xr.at[3], {"tok": xn})
    two_a.start()
    two_b.start()
    lax.fori_loop(2, 4, launch, 0)
    pass_on(1)
    feed(1)
    pass_on(2)
    feed(2)
    for b in range(bricks):
        pmsg[b] = part[pl.ds(pl.multiple_of(b * per + other * half, half), half), :].astype(BF16)
    swap_part = remote(pmsg, pbox, xs.at[4], xr.at[4], {"mdl": other})
    swap_part.start()
    two_a.wait()
    two_b.wait()
    s2[:, :, 0:cut] = (s1a[:, y].astype(F32) + g2a[...].astype(F32)).astype(BF16)
    s2[:, :, cut : 2 * cut] = (s1b[:, x].astype(F32) + g2b[...].astype(F32)).astype(BF16)
    last = []
    for d in range(1, 4):
        copy = remote(
            s2.at[lax.rem(z + d, 4)], g3.at[d - 1], xs.at[5 + d], xr.at[5 + d],
            {"tok": lax.rem(me + 4 * d, count)},
        )
        copy.start()
        last.append(copy)
    pass_on(3)
    swap_part.wait()
    for q in (1, 2, 3):
        plane_copy(q, 0).wait()

    def settle(b, c):
        at = pl.ds(pl.multiple_of(b * per + core * half, half), half)
        result[b] = part[at, :] + pbox[b].astype(F32) + merge(0, b)
        return c

    lax.fori_loop(0, bricks, settle, 0)
    for j in range(1, 4):
        z_copy(j).wait()
    result[...] = result[...] + zbox[0].astype(F32) + zbox[1].astype(F32) + zbox[2].astype(F32)
    for b in range(bricks):
        v = tok[b, mine, :].astype(F32)
        inv = lax.rsqrt(jnp.mean(v * v, axis=-1, keepdims=True) + norm_eps)
        normed = v * inv
        g = result[b] * gain[...]
        base = gout[pl.ds(pl.multiple_of(b * per + core * half, half), half), :].astype(F32)
        out[b, mine, :] = (
            base + inv * (g - normed * jnp.mean(g * normed, axis=-1, keepdims=True))
        ).astype(BF16)
    share = remote(out.at[:, mine, :], out.at[:, mine, :], xs.at[5], xr.at[5], {"mdl": other})
    share.start()
    for copy in last:
        copy.wait()
    gw_out[...] = (
        s2[z].astype(F32) + g3[0].astype(F32) + g3[1].astype(F32) + g3[2].astype(F32)
    )
    share.wait_send()
    remote(out.at[:, theirs, :], out.at[:, theirs, :], xs.at[5], xr.at[5], {"mdl": other}).wait_recv()


def body(
    tokens,
    cotangent,
    norm_gain,
    w_qkv,
    w_out,
    w_up,
    w_down,
    w_disp,
    rel_bias,
    face_source,
    face_live,
    send_bricks,
):
    bricks, per, width = tokens.shape
    rows = bricks * per
    heads = rel_bias.shape[0]
    dh = w_out.shape[0] // heads
    faces = face_source.shape[1]
    devices = lax.axis_size("tok")
    slots = send_bricks.shape[2]
    total = devices * slots
    kv = heads * 2 * dh
    wide = heads * 3 * dh
    span = (faces + 1) * per
    ff = w_up.shape[1]
    half = per // 2
    send = send_bricks.reshape(-1)
    row = jnp.zeros((8, 128), jnp.int32).at[0, : devices * slots].set(send)
    sources = face_source.reshape(-1)
    matches = (sources[:, None] == sources[None, :]).astype(jnp.int32)
    count = sources.shape[0]
    before = jnp.arange(count)[None, :] < jnp.arange(count)[:, None]
    arrival = sources * slots + jnp.sum(jnp.where(before, matches, 0), axis=1)
    seen = jnp.concatenate([jnp.ones((bricks, 1), jnp.int32), face_live], axis=1)
    seen = jnp.repeat(seen, per, axis=1)
    gain = norm_gain.reshape(1, width)
    flat = tokens.reshape(rows, width)
    any_spec = pl.BlockSpec(memory_space=pl.ANY)
    dma = pltpu.SemaphoreType.DMA

    def shape(dims, kind=BF16):
        return jax.ShapeDtypeStruct(dims, kind)

    def talk(ident, room):
        return pltpu.CompilerParams(
            vmem_limit_bytes=room << 20, collective_id=ident, has_side_effects=True
        )

    small = pltpu.CompilerParams(vmem_limit_bytes=10 << 20)

    recv, hidden, packed, up_pre, part_ffn, table = pl.pallas_call(
        functools.partial(gather_kernel, devices),
        out_shape=(
            shape((devices, slots, per, width)),
            shape((rows, width)),
            shape((rows, wide)),
            shape((rows, ff), F32),
            shape((rows, width), F32),
            shape((devices, 8, 128), jnp.int32),
        ),
        in_specs=[SM, VM, VM, VM, any_spec, any_spec, any_spec],
        out_specs=(VM,) * 6,
        scratch_shapes=[
            pltpu.VMEM((devices - 1, slots, half, width), BF16),
            pltpu.VMEM((width, wide), BF16),
            pltpu.VMEM((width, ff), BF16),
            pltpu.VMEM((ff, width), BF16),
            dma((3,)),
            dma((devices - 1,)),
            dma((devices - 1,)),
            dma((devices - 1,)),
            dma((devices - 1,)),
            dma((devices - 1,)),
            dma((devices - 1,)),
        ],
        compiler_params=talk(2, 48),
        name="gather",
    )(send, tokens, gain, row, w_qkv, w_up, w_down)

    attended, probs, window, hid = pl.pallas_call(
        functools.partial(attend_kernel, heads, dh, per, faces),
        out_shape=(
            shape((rows, heads * dh)),
            shape((bricks * heads, per, span), F32),
            shape((bricks, span, kv)),
            shape((bricks, span, width)),
        ),
        in_specs=[SM] + [VM] * 7,
        out_specs=(VM,) * 4,
        scratch_shapes=[pltpu.VMEM((faces * per, width), BF16)],
        compiler_params=small,
        name="attend",
    )(arrival, hidden, packed, recv.reshape(total, per, width), gain, w_qkv, rel_bias, seen)

    part_out = part_ffn + jnp.dot(attended, w_out, preferred_element_type=F32)
    folding, grad_out = pl.pallas_call(
        fold_swap_kernel,
        out_shape=(shape((1, rows), F32), shape((rows, width))),
        in_specs=[VM] * 4,
        out_specs=(VM, VM),
        scratch_shapes=[pltpu.VMEM((rows, width), F32), dma, dma],
        compiler_params=talk(0, 8),
        name="fold_swap",
    )(flat, part_out, cotangent.reshape(rows, width), w_disp)
    grad_mixed = jnp.dot(grad_out, w_out.T, preferred_element_type=F32).astype(BF16)

    own, ret, gw = pl.pallas_call(
        functools.partial(attend_back_kernel, heads, dh, per, faces),
        out_shape=(
            shape((rows, width), F32),
            shape((total, per, width)),
            shape((width, wide)),
        ),
        in_specs=[SM] + [VM] * 6,
        out_specs=(VM,) * 3,
        scratch_shapes=[pltpu.VMEM((span, wide), BF16), pltpu.VMEM((width, wide), F32)],
        compiler_params=small,
        name="attend_back",
    )(arrival, packed, window, hid, probs, grad_mixed, w_qkv)

    piece = width // devices
    cut = wide // 2
    grad_tokens, grad_weight = pl.pallas_call(
        functools.partial(return_kernel, devices),
        out_shape=(shape((bricks, per, width)), shape((piece, wide), F32)),
        in_specs=[SM] + [VM] * 7 + [any_spec] * 2,
        out_specs=(VM, VM),
        scratch_shapes=[
            pltpu.VMEM((devices, slots, half, width), BF16),
            pltpu.VMEM((devices, slots, half, width), BF16),
            pltpu.VMEM((devices, slots, half, width), BF16),
            pltpu.VMEM((rows, width), F32),
            pltpu.VMEM((bricks, half, width), BF16),
            pltpu.VMEM((bricks, half, width), BF16),
            pltpu.VMEM((bricks, half, width), F32),
            pltpu.VMEM((4, 2, piece, cut), BF16),
            pltpu.VMEM((4, 2, piece, cut), BF16),
            pltpu.VMEM((4, 2, piece, cut), BF16),
            pltpu.VMEM((4, 2, piece, cut), BF16),
            pltpu.VMEM((4, piece, cut), BF16),
            pltpu.VMEM((4, piece, cut), BF16),
            pltpu.VMEM((4, piece, wide), BF16),
            pltpu.VMEM((3, piece, wide), BF16),
            pltpu.VMEM((width, ff), BF16),
            pltpu.VMEM((ff, width), BF16),
            pltpu.VMEM((3, bricks, half, width), BF16),
            pltpu.VMEM((3, bricks, half, width), BF16),
            dma((2,)),
            dma((devices,)),
            dma((devices,)),
            dma((devices,)),
            dma((devices,)),
            dma((9,)),
            dma((9,)),
            dma((3,)),
            dma((3,)),
        ],
        compiler_params=talk(1, 48),
        name="give_back",
    )(
        table[:, 0, : devices * slots].reshape(-1),
        tokens,
        gain,
        grad_out,
        own,
        ret.reshape(devices, slots, per, width),
        gw.reshape(4, 2, 2, piece, wide),
        up_pre,
        w_up,
        w_down,
    )
    return (folding.reshape(bricks, per), grad_tokens, grad_weight)


def solution(mesh):
    return jax.shard_map(
        body if mesh.shape["tok"] == 16 and mesh.shape["mdl"] == 2 else body_wide,
        mesh=mesh,
        in_specs=(
            P("tok", None, None),
            P("tok", None, None),
            P(),
            P(None, "mdl"),
            P("mdl", None),
            P(None, "mdl"),
            P("mdl", None),
            P(),
            P("mdl", None, None),
            P("tok", None),
            P("tok", None),
            P("tok", None, None),
        ),
        out_specs=(P("tok", None), P("tok", None, None), P("tok", "mdl")),
        check_vma=False,
    )
```
